32 devices in a mesh: tm: 4 (over x, core), rows: 8 (over z, y).
Axes of the slice: x: 2, y: 2, z: 4, core: 2. Of those that a mesh axis runs over, the one named last changes fastest.
Arguments:
- latent: bfloat16 [16, 192, 32, 128], P('tm', None, 'rows'), may hold values from -6 to 6
- clip_ids: int32 [16], replicated, may hold values from 0 to 1, as said below
- gain_in: float32 [192], replicated, may hold values from 0.1 to 1.9
- conv_in: bfloat16 [3, 3, 3, 96, 192], replicated, may hold values from -0.078125 to 0.078125
- bias_in: float32 [96], replicated, may hold values from -3 to 3
- gain_mid: float32 [96], replicated, may hold values from 0.1 to 1.9
- conv_mid: bfloat16 [3, 3, 3, 96, 96], replicated, may hold values from -0.125 to 0.125
- bias_mid: float32 [96], replicated, may hold values from -3 to 3
- skip_weight: bfloat16 [96, 192], replicated, may hold values from -0.4375 to 0.4375
- skip_bias: float32 [96], replicated, may hold values from -3 to 3
Outputs:
- decoded: bfloat16 [16, 96, 32, 128], P('tm', None, 'rows')
The draws below stay inside these ranges and needn't reach their ends.
Inputs may be any that keep to these rules, and one draw needn't show every extreme that they name: `clip_ids`: clip number of each frame; numbers never fall along the frames and every number appears; each clip lies on consecutive frames, and every clip other than the window's first and last holds 1 + 4 k frames, at most 21.
All inputs are finite; a program needn't handle non-finite values.
Results may differ from the reference program's by a relative error of at most 0.0075.
Values may be sent and summed in bfloat16 or wider, within the bound.
No kernel may reach another device: no remote copies, remote signals or barrier semaphores. Data moves between devices by JAX's collectives and lax.ppermute only.
A program may use at most 64 MiB of HBM per device.

```python
import jax
import jax.numpy as jnp
from jax import lax

CIN = 192
COUT = 96
WIDTH = 128
FRAMES = 16
HEIGHT = 32
CLIPS = 2


def draw_clip_ids(key, part):
    inner_count = max(CLIPS - 2, 1)
    step_most = min(5, ((FRAMES - 2) // inner_count - 1) // 4)
    first_key = jax.random.fold_in(key, 11)
    second_key = jax.random.fold_in(key, 23)
    quarter_steps = jax.random.randint(first_key, (CLIPS - 2,), 0, step_most + 1, dtype=jnp.int32)
    lengths = 1 + 4 * quarter_steps
    remain = FRAMES - jnp.sum(lengths)
    opening = jax.random.randint(second_key, (), 1, remain, dtype=jnp.int32)
    bounds = opening + jnp.concatenate([jnp.zeros((1,), jnp.int32), jnp.cumsum(lengths).astype(jnp.int32)])
    frames = jnp.arange(FRAMES, dtype=jnp.int32)
    return jnp.sum((frames[:, None] >= bounds[None, :]).astype(jnp.int32), axis=1).astype(jnp.int32)


def shard_levels(key, extent, split, low, top_value):
    def one(axis_at, parts):
        draws = jax.random.uniform(jax.random.fold_in(jax.random.fold_in(key, 6), axis_at), (parts,), jnp.float32, low / len(split), top_value / len(split))
        return jnp.repeat(jnp.exp(draws), extent[axis_at] // parts).reshape((-1,) + (1,) * (len(extent) - axis_at - 1))

    level = one(*split[0])
    for cut in split[1:]:
        level = level * one(*cut)
    return level


def centred(key, dims, spread, limit, split=(), kind=jnp.bfloat16):
    array = spread * jax.random.normal(key, dims, jnp.float32)
    if split:
        array = array * shard_levels(key, dims, split, -0.22, 0.18)
    return jnp.clip(array, -limit, limit).astype(kind)


def setup_inputs(seed: int = 0) -> dict:
    seeds = jax.random.split(jax.random.key(seed), 11)
    latent = centred(seeds[0], (FRAMES, CIN, HEIGHT, WIDTH), 1.0, 6.0, ((0, 4), (2, 8)))
    clip_ids = draw_clip_ids(jax.random.fold_in(seeds[10], 71), 0)
    gain_in = jnp.clip(1.0 + 0.18 * jax.random.normal(seeds[2], (CIN,), jnp.float32), 0.1, 1.9)
    conv_in = centred(seeds[3], (3, 3, 3, COUT, CIN), (27 * CIN) ** -0.5, 0.078125)
    bias_in = centred(seeds[4], (COUT,), 0.5, 3.0, (), jnp.float32)
    gain_mid = jnp.clip(1.0 + 0.18 * jax.random.normal(seeds[5], (COUT,), jnp.float32), 0.1, 1.9)
    conv_mid = centred(seeds[6], (3, 3, 3, COUT, COUT), (27 * COUT) ** -0.5, 0.125)
    bias_mid = centred(seeds[7], (COUT,), 0.5, 3.0, (), jnp.float32)
    skip_weight = centred(seeds[8], (COUT, CIN), CIN ** -0.5, 0.4375)
    skip_bias = centred(seeds[9], (COUT,), 0.5, 3.0, (), jnp.float32)
    return {"latent": latent, "clip_ids": clip_ids, "gain_in": gain_in, "conv_in": conv_in, "bias_in": bias_in, "gain_mid": gain_mid, "conv_mid": conv_mid, "bias_mid": bias_mid, "skip_weight": skip_weight, "skip_bias": skip_bias}


def keep_table(clip_ids, start, count):
    frames = start + jnp.arange(count, dtype=jnp.int32)
    final_index = clip_ids.shape[0] - 1
    own_clip = jnp.take(clip_ids, jnp.clip(frames, 0, final_index))
    tables = []
    for back_step in range(3):
        source = frames - back_step
        src_clip = jnp.take(clip_ids, jnp.clip(source, 0, final_index))
        tables.append(((source >= 0) & (src_clip == own_clip)).astype(jnp.float32))
    return jnp.stack(tables)

def norm_silu(values, gain):
    floats = values.astype(jnp.float32)
    mean_sq = lax.optimization_barrier(jnp.mean(floats * floats, axis=1, keepdims=True))
    scaled = floats * lax.rsqrt(mean_sq + 1e-06) * gain[None, :, None, None]
    return jax.nn.silu(scaled).astype(jnp.bfloat16)

def causal_conv(padded, weight, keep, out_frames, out_rows):
    wide = jnp.pad(padded, ((0, 0), (0, 0), (0, 0), (1, 1)))
    width_all = padded.shape[3]
    total = jnp.zeros((out_frames, weight.shape[3], out_rows, width_all), jnp.float32)
    for t_tap in range(3):
        part = jnp.zeros_like(total)
        for h_tap in range(3):
            for w_tap in range(3):
                slab = wide[t_tap:t_tap + out_frames, :, h_tap:h_tap + out_rows, w_tap:w_tap + width_all]
                part = part + jnp.einsum('oc,fcrw->forw', weight[t_tap, h_tap, w_tap].astype(jnp.float32), slab.astype(jnp.float32))
        total = total + part * keep[2 - t_tap][:, None, None, None]
    return total

def reference(latent, clip_ids, gain_in, conv_in, bias_in, gain_mid, conv_mid, bias_mid, skip_weight, skip_bias):
    frames_all = latent.shape[0]
    height_all = latent.shape[2]
    keep = keep_table(clip_ids, 0, frames_all)
    first = norm_silu(latent, gain_in)
    first_pad = jnp.pad(first, ((2, 0), (0, 0), (1, 1), (0, 0)))

    def layer_one(index):
        window = lax.dynamic_slice_in_dim(first_pad, index, 3, 0)
        mask = lax.dynamic_slice_in_dim(keep, index, 1, 1)
        result = causal_conv(window, conv_in, mask, 1, height_all)[0]
        return (result + bias_in[:, None, None]).astype(jnp.bfloat16)
    hidden = lax.map(layer_one, jnp.arange(frames_all, dtype=jnp.int32))
    second = norm_silu(hidden, gain_mid)
    second_pad = jnp.pad(second, ((2, 0), (0, 0), (1, 1), (0, 0)))

    def layer_two(index):
        window = lax.dynamic_slice_in_dim(second_pad, index, 3, 0)
        mask = lax.dynamic_slice_in_dim(keep, index, 1, 1)
        tail = causal_conv(window, conv_mid, mask, 1, height_all)[0]
        frame = lax.dynamic_index_in_dim(latent, index, 0, keepdims=False)
        short = jnp.einsum('oc,crw->orw', skip_weight.astype(jnp.float32), frame.astype(jnp.float32))
        return (tail + bias_mid[:, None, None] + short + skip_bias[:, None, None]).astype(jnp.bfloat16)
    return lax.map(layer_two, jnp.arange(frames_all, dtype=jnp.int32))
```

```python
import jax
import jax.numpy as jnp
from jax import lax
from jax.experimental import pallas as pl
from jax.experimental.pallas import tpu as pltpu
from jax.sharding import PartitionSpec as P

F32 = jnp.float32
BF16 = jnp.bfloat16
VMEM = pl.BlockSpec(memory_space=pltpu.VMEM)
SMEM = pl.BlockSpec(memory_space=pltpu.SMEM)


def silu_norm(values, gain):
    mean_sq = jnp.mean(values * values, axis=0, keepdims=True)
    scaled = values * lax.rsqrt(mean_sq + 1e-06) * gain
    return scaled / (1.0 + jnp.exp(-scaled))


def column_taps(act):
    lane = lax.broadcasted_iota(jnp.int32, act.shape, 1)
    width = act.shape[1]
    left = jnp.where(lane == 0, 0.0, pltpu.roll(act, 1, 1))
    right = jnp.where(lane == width - 1, 0.0, pltpu.roll(act, width - 1, 1))
    return left.astype(BF16), act.astype(BF16), right.astype(BF16)


def spread(vector, width):
    return jnp.broadcast_to(vector, (width, vector.shape[1])).T


def kept(clip_ref, frame, back):
    final = clip_ref.shape[0] - 1
    here = clip_ref[jnp.clip(frame, 0, final)]
    there = clip_ref[jnp.clip(frame - back, 0, final)]
    return (frame - back >= 0) & (here == there)


def fold_taps(weight_ref, row_tap, first, last):
    return jnp.concatenate([weight_ref[t, row_tap, j] for t in range(first, last + 1) for j in range(3)], axis=1)


def dot(a, b):
    return jnp.dot(a, b, preferred_element_type=F32)


def by_suffix(clip_ref, frame, first, last, body, nothing):
    flags = [None if t == 2 else kept(clip_ref, frame, 2 - t) for t in range(first, last + 1)]
    prior = None
    for t, flag in zip(range(first, last + 1), flags):
        here = flag if prior is None else (~prior if flag is None else ~prior & flag)
        if here is None:
            body(t)
            return
        pl.when(here)(lambda t=t: body(t))
        prior = flag
    if last != 2:
        pl.when(~prior)(nothing)


def conv_first(xs_ref, wt_ref, wu_ref, clip_ref, start, columns, frames, emit):
    depth = xs_ref.shape[0] // frames
    for out in range(frames + 2):
        first, last = max(0, 2 - out), min(2, frames + 1 - out)

        def body(t, out=out, last=last):
            rows = pl.ds((out - 2 + t) * depth, (last + 1 - t) * depth)
            if t == 1:
                weight = wu_ref[:, : (last + 1 - t) * depth]
            else:
                weight = wt_ref[:, t * depth : (last + 1) * depth]
            emit(out, dot(weight, xs_ref[rows, columns]))

        def nothing(out=out):
            emit(out, jnp.zeros((wt_ref.shape[0], columns.size), F32))

        by_suffix(clip_ref, start + out, first, last, body, nothing)


def first_kernel(clip_ref, lat_ref, weight_ref, gain_ref, xs_ref, wt_ref, wu_ref, up_ref, edge_ref):
    frames, chans, pixels = lat_ref.shape
    outs = weight_ref.shape[3]
    width = up_ref.shape[2] // 2
    height = pixels // width
    start = lax.axis_index("tm") * frames
    gain = spread(gain_ref[...], width)
    for i in range(3):
        wt_ref[i * outs : (i + 1) * outs, :] = fold_taps(weight_ref, i, 0, 2)
        wu_ref[i * outs : (i + 1) * outs, :] = fold_taps(weight_ref, i, 1, 2)
    for f in range(frames):
        for r in range(height):
            cols = pl.ds(r * width, width)
            act = silu_norm(lat_ref[f, :, cols].astype(F32), gain)
            for j, tap in enumerate(column_taps(act)):
                xs_ref[pl.ds((f * 3 + j) * chans, chans), cols] = tap

    def emit(out, y):
        y0, y1, y2 = (y[i * outs : (i + 1) * outs] for i in range(3))
        far = y0[:, :width] + y1[:, width:]
        up_ref[out, :, :width] = far.astype(BF16)
        up_ref[out, :, width:] = y0[:, width:].astype(BF16)
        edge_ref[out, :, :width] = y2[:, :width]
        edge_ref[out, :, width : 2 * width] = y1[:, :width] + y2[:, width:]
        edge_ref[out, :, 2 * width :] = far

    conv_first(xs_ref, wt_ref, wu_ref, clip_ref, start, pl.ds(pixels - 2 * width, 2 * width), frames, emit)


def inner_kernel(clip_ref, xs_ref, wt_ref, wu_ref, edge_ref, part_ref):
    width = edge_ref.shape[2] // 3
    outs = edge_ref.shape[1]
    frames = edge_ref.shape[0] - 2
    inner = part_ref.shape[2] // width - 3
    start = lax.axis_index("tm") * frames

    def emit(out, y):
        y0, y1, y2 = (y[i * outs : (i + 1) * outs] for i in range(3))
        for h in range(-1, inner + 2):
            total = None
            for tap, row in ((y0, h - 1), (y1, h), (y2, h + 1)):
                if 0 <= row < inner:
                    term = tap[:, row * width : (row + 1) * width]
                    total = term if total is None else total + term
            if h >= inner - 1:
                e = h - inner + 1
                term = edge_ref[out, :, e * width : (e + 1) * width]
                total = term if total is None else total + term
            part_ref[out, :, (h + 1) * width : (h + 2) * width] = total

    conv_first(xs_ref, wt_ref, wu_ref, clip_ref, start, pl.ds(0, inner * width), frames, emit)


def act_rows(total, h, height, bias, gain):
    hidden = (total + bias).astype(BF16).astype(F32)
    act = silu_norm(hidden, gain)
    if h == -1:
        return jnp.where(lax.axis_index("rows") > 0, act, 0.0)
    if h == height - 1:
        return jnp.where(lax.axis_index("rows") == lax.axis_size("rows") - 1, act, 0.0)
    return act


def hidden_sum(part_ref, got_ref, out, h, width):
    total = part_ref[out, :, (h + 1) * width : (h + 2) * width]
    if h < 1:
        total = total + got_ref[out, :, (h + 1) * width : (h + 2) * width].astype(F32)
    return total


def later_kernel(part_ref, got_ref, bias_ref, gain_ref, msg_ref):
    width = got_ref.shape[2] // 2
    frames = part_ref.shape[0] - 2
    height = part_ref.shape[2] // width - 1
    bias, gain = spread(bias_ref[...], width), spread(gain_ref[...], width)
    for k in range(4):
        for h in range(-1, height):
            total = hidden_sum(part_ref, got_ref, frames - 2 + k, h, width)
            cols = pl.ds((h + 1) * width, width)
            if k < 2:
                total = act_rows(total, h, height, bias, gain)
            msg_ref[k, :, cols] = total.astype(BF16)


def conv_second(xs_ref, wt_refs, clip_ref, start, columns, frames, emit):
    depth = xs_ref.shape[0] // (frames + 2)
    for out in range(frames):

        def body(t, out=out):
            rows = pl.ds((out + t) * depth, (3 - t) * depth)
            emit(out, dot(wt_refs[t][...], xs_ref[rows, columns]))

        by_suffix(clip_ref, start + out, 0, 2, body, None)


def second_kernel(clip_ref, part_ref, got_ref, mine_ref, before_ref, weight_ref, bias_ref, gain_ref, xs_ref, w0_ref, w1_ref, w2_ref, down_ref, edge_ref):
    width = got_ref.shape[2] // 2
    frames = part_ref.shape[0] - 2
    height = part_ref.shape[2] // width - 1
    outs = part_ref.shape[1]
    start = lax.axis_index("tm") * frames
    bias, gain = spread(bias_ref[...], width), spread(gain_ref[...], width)
    refs = (w0_ref, w1_ref, w2_ref)
    for t, ref in enumerate(refs):
        for i in range(3):
            ref[i * outs : (i + 1) * outs, :] = fold_taps(weight_ref, i, t, 2)
    for s in range(-2, frames):
        for h in range(-1, height):
            cols = pl.ds((h + 1) * width, width)
            if s < 0:
                act = before_ref[s + 2, :, cols].astype(F32)
            elif s >= frames - 2:
                act = mine_ref[s - frames + 2, :, cols].astype(F32)
            else:
                total = hidden_sum(part_ref, got_ref, s, h, width)
                if s < 2:
                    total = total + before_ref[2 + s, :, cols].astype(F32)
                act = act_rows(total, h, height, bias, gain)
            for j, tap in enumerate(column_taps(act)):
                xs_ref[pl.ds(((s + 2) * 3 + j) * outs, outs), cols] = tap

    def emit(out, y):
        y0, y1, y2 = (y[i * outs : (i + 1) * outs] for i in range(3))
        down_ref[out, :, :width] = y2[:, :width].astype(BF16)
        down_ref[out, :, width:] = (y1[:, :width] + y2[:, width:]).astype(BF16)
        edge_ref[out, :, :width] = y0[:, :width] + y1[:, width:]
        edge_ref[out, :, width:] = y0[:, width:]

    conv_second(xs_ref, refs, clip_ref, start, pl.ds(0, 2 * width), frames, emit)


def last_kernel(clip_ref, xs_ref, w0_ref, w1_ref, w2_ref, edge_ref, lat_ref, skip_ref, bias_ref, skip_bias_ref, out_ref):
    width = edge_ref.shape[2] // 2
    frames, outs, pixels = out_ref.shape
    height = pixels // width
    start = lax.axis_index("tm") * frames
    bias = spread(bias_ref[...] + skip_bias_ref[...], width)
    refs = (w0_ref, w1_ref, w2_ref)
    skip = skip_ref[...]

    def emit(out, y):
        y0, y1, y2 = (y[i * outs : (i + 1) * outs] for i in range(3))
        short = dot(skip, lat_ref[out])
        for r in range(height):
            total = short[:, r * width : (r + 1) * width] + bias
            for tap, row in ((y0, r - 1), (y1, r), (y2, r + 1)):
                if 1 <= row < height:
                    total = total + tap[:, (row - 1) * width : row * width]
            if r < 2:
                total = total + edge_ref[out, :, r * width : (r + 1) * width]
            out_ref[out, :, r * width : (r + 1) * width] = total

    conv_second(xs_ref, refs, clip_ref, start, pl.ds(2 * width, (height - 1) * width), frames, emit)


def call(kernel, shapes, operands, flops, smem=0):
    moved = sum(x.size * x.dtype.itemsize for x in operands) + sum(s.size * s.dtype.itemsize for s in shapes)
    single = len(shapes) == 1
    return pl.pallas_call(
        kernel,
        out_shape=shapes[0] if single else tuple(shapes),
        in_specs=[SMEM] * smem + [VMEM] * (len(operands) - smem),
        out_specs=VMEM if single else tuple(VMEM for _ in shapes),
        cost_estimate=pl.CostEstimate(flops=flops, bytes_accessed=moved, transcendentals=0),
    )(*operands)


def moved_by(block, axis, distance):
    devices = range(lax.axis_size(axis))
    return lax.ppermute(block, axis, [(i, i + distance) for i in devices if i + distance in devices])


def shards(latent, clip_ids, gain_in, conv_in, bias_in, gain_mid, conv_mid, bias_mid, skip_weight, skip_bias):
    frames, chans, height, width = latent.shape
    outs = conv_in.shape[3]
    shape = jax.ShapeDtypeStruct
    lat = latent.reshape(frames, chans, height * width)
    row = lambda v: v.reshape(1, -1)
    deep, deep_mid, tall = 3 * chans, 3 * outs, 3 * outs
    work = 2 * tall * 3 * deep * frames * width
    xs, wt, wu, up, edge = call(
        first_kernel,
        [
            shape((frames * deep, height * width), BF16),
            shape((tall, 3 * deep), BF16),
            shape((tall, 2 * deep), BF16),
            shape((frames + 2, outs, 2 * width), BF16),
            shape((frames + 2, outs, 3 * width), F32),
        ],
        (clip_ids, lat, conv_in, row(gain_in)),
        work * 2,
        1,
    )
    got = moved_by(up, "rows", 1)
    part = call(
        inner_kernel,
        [shape((frames + 2, outs, (height + 1) * width), F32)],
        (clip_ids, xs, wt, wu, edge),
        work * (height - 2),
        1,
    )
    msg = call(
        later_kernel,
        [shape((4, outs, (height + 1) * width), BF16)],
        (part, got, row(bias_in), row(gain_mid)),
        1000,
    )
    before = moved_by(msg, "tm", 1)
    xs_mid, w0, w1, w2, down, edge_mid = call(
        second_kernel,
        [
            shape(((frames + 2) * deep_mid, (height + 1) * width), BF16),
            shape((tall, 3 * deep_mid), BF16),
            shape((tall, 2 * deep_mid), BF16),
            shape((tall, deep_mid), BF16),
            shape((frames, outs, 2 * width), BF16),
            shape((frames, outs, 2 * width), F32),
        ],
        (clip_ids, part, got, msg, before, conv_mid, row(bias_in), row(gain_mid)),
        work,
        1,
    )
    below = moved_by(down, "rows", -1)
    total = call(
        last_kernel,
        [shape((frames, outs, height * width), F32)],
        (clip_ids, xs_mid, w0, w1, w2, edge_mid, lat, skip_weight, row(bias_mid), row(skip_bias)),
        work * (height - 2) // 2,
        1,
    )
    tail = total[:, :, (height - 2) * width :] + below.astype(F32)
    result = jnp.concatenate([total[:, :, : (height - 2) * width], tail], axis=2)
    return result.astype(BF16).reshape(frames, outs, height, width)


def solution(mesh):
    return jax.shard_map(
        shards,
        mesh=mesh,
        in_specs=(P("tm", None, "rows", None), P(), P(), P(), P(), P(), P(), P(), P(), P()),
        out_specs=P("tm", None, "rows", None),
        check_vma=False,
    )
```

```python
import jax
import jax.numpy as jnp
from jax import lax
from jax.experimental import pallas as pl
from jax.experimental.pallas import tpu as pltpu
from jax.sharding import PartitionSpec as P

F32 = jnp.float32
BF16 = jnp.bfloat16
VMEM = pl.BlockSpec(memory_space=pltpu.VMEM)
SMEM = pl.BlockSpec(memory_space=pltpu.SMEM)


def silu_norm(values, gain):
    mean_sq = jnp.mean(values * values, axis=0, keepdims=True)
    scaled = values * lax.rsqrt(mean_sq + 1e-06) * gain
    return scaled / (1.0 + jnp.exp(-scaled))


def column_taps(act):
    lane = lax.broadcasted_iota(jnp.int32, act.shape, 1)
    width = act.shape[1]
    left = jnp.where(lane == 0, 0.0, pltpu.roll(act, 1, 1))
    right = jnp.where(lane == width - 1, 0.0, pltpu.roll(act, width - 1, 1))
    return left.astype(BF16), act.astype(BF16), right.astype(BF16)


def spread(vector, width):
    return jnp.broadcast_to(vector, (width, vector.shape[1])).T


def kept(clip_ref, frame, back):
    final = clip_ref.shape[0] - 1
    here = clip_ref[jnp.clip(frame, 0, final)]
    there = clip_ref[jnp.clip(frame - back, 0, final)]
    return (frame - back >= 0) & (here == there)


def fold_taps(weight_ref, row_tap, first, last):
    return jnp.concatenate([weight_ref[t, row_tap, j] for t in range(first, last + 1) for j in range(3)], axis=1)


def dot(a, b):
    return jnp.dot(a, b, preferred_element_type=F32)


def by_suffix(clip_ref, frame, first, last, body, nothing):
    flags = [None if t == 2 else kept(clip_ref, frame, 2 - t) for t in range(first, last + 1)]
    prior = None
    for t, flag in zip(range(first, last + 1), flags):
        here = flag if prior is None else (~prior if flag is None else ~prior & flag)
        if here is None:
            body(t)
            return
        pl.when(here)(lambda t=t: body(t))
        prior = flag
    if last != 2:
        pl.when(~prior)(nothing)


def conv_first(xs_ref, wt_ref, wu_ref, clip_ref, start, columns, frames, emit):
    depth = xs_ref.shape[0] // frames
    for out in range(frames + 2):
        first, last = max(0, 2 - out), min(2, frames + 1 - out)

        def body(t, out=out, last=last):
            rows = pl.ds((out - 2 + t) * depth, (last + 1 - t) * depth)
            if t == 1:
                weight = wu_ref[:, : (last + 1 - t) * depth]
            else:
                weight = wt_ref[:, t * depth : (last + 1) * depth]
            emit(out, dot(weight, xs_ref[rows, columns]))

        def nothing(out=out):
            emit(out, jnp.zeros((wt_ref.shape[0], columns.size), F32))

        by_suffix(clip_ref, start + out, first, last, body, nothing)


def first_kernel(clip_ref, lat_ref, weight_ref, gain_ref, xs_ref, wt_ref, wu_ref, up_ref, edge_ref):
    frames, chans, pixels = lat_ref.shape
    outs = weight_ref.shape[3]
    width = up_ref.shape[2] // 2
    height = pixels // width
    start = lax.axis_index("tm") * frames
    gain = spread(gain_ref[...], width)
    for i in range(3):
        wt_ref[i * outs : (i + 1) * outs, :] = fold_taps(weight_ref, i, 0, 2)
        wu_ref[i * outs : (i + 1) * outs, :] = fold_taps(weight_ref, i, 1, 2)
    for f in range(frames):
        for r in range(height):
            cols = pl.ds(r * width, width)
            act = silu_norm(lat_ref[f, :, cols].astype(F32), gain)
            for j, tap in enumerate(column_taps(act)):
                xs_ref[pl.ds((f * 3 + j) * chans, chans), cols] = tap

    def emit(out, y):
        y0, y1, y2 = (y[i * outs : (i + 1) * outs] for i in range(3))
        far = y0[:, :width] + y1[:, width:]
        up_ref[out, :, :width] = far.astype(BF16)
        up_ref[out, :, width:] = y0[:, width:].astype(BF16)
        edge_ref[out, :, :width] = y2[:, :width]
        edge_ref[out, :, width : 2 * width] = y1[:, :width] + y2[:, width:]
        edge_ref[out, :, 2 * width :] = far

    conv_first(xs_ref, wt_ref, wu_ref, clip_ref, start, pl.ds(pixels - 2 * width, 2 * width), frames, emit)


def inner_kernel(clip_ref, xs_ref, wt_ref, wu_ref, edge_ref, part_ref):
    width = edge_ref.shape[2] // 3
    outs = edge_ref.shape[1]
    frames = edge_ref.shape[0] - 2
    inner = part_ref.shape[2] // width - 3
    start = lax.axis_index("tm") * frames

    def emit(out, y):
        y0, y1, y2 = (y[i * outs : (i + 1) * outs] for i in range(3))
        for h in range(-1, inner + 2):
            total = None
            for tap, row in ((y0, h - 1), (y1, h), (y2, h + 1)):
                if 0 <= row < inner:
                    term = tap[:, row * width : (row + 1) * width]
                    total = term if total is None else total + term
            if h >= inner - 1:
                e = h - inner + 1
                term = edge_ref[out, :, e * width : (e + 1) * width]
                total = term if total is None else total + term
            part_ref[out, :, (h + 1) * width : (h + 2) * width] = total

    conv_first(xs_ref, wt_ref, wu_ref, clip_ref, start, pl.ds(0, inner * width), frames, emit)


def act_rows(total, h, height, bias, gain):
    hidden = (total + bias).astype(BF16).astype(F32)
    act = silu_norm(hidden, gain)
    if h == -1:
        return jnp.where(lax.axis_index("rows") > 0, act, 0.0)
    if h == height - 1:
        return jnp.where(lax.axis_index("rows") == lax.axis_size("rows") - 1, act, 0.0)
    return act


def hidden_sum(part_ref, got_ref, out, h, width):
    total = part_ref[out, :, (h + 1) * width : (h + 2) * width]
    if h < 1:
        total = total + got_ref[out, :, (h + 1) * width : (h + 2) * width].astype(F32)
    return total


def later_kernel(part_ref, got_ref, bias_ref, gain_ref, msg_ref):
    width = got_ref.shape[2] // 2
    frames = part_ref.shape[0] - 2
    height = part_ref.shape[2] // width - 1
    bias, gain = spread(bias_ref[...], width), spread(gain_ref[...], width)
    for k in range(4):
        for h in range(-1, height):
            total = hidden_sum(part_ref, got_ref, frames - 2 + k, h, width)
            cols = pl.ds((h + 1) * width, width)
            if k < 2:
                total = act_rows(total, h, height, bias, gain)
            msg_ref[k, :, cols] = total.astype(BF16)


def conv_second(xs_ref, wt_refs, clip_ref, start, columns, frames, emit):
    depth = xs_ref.shape[0] // (frames + 2)
    for out in range(frames):

        def body(t, out=out):
            rows = pl.ds((out + t) * depth, (3 - t) * depth)
            emit(out, dot(wt_refs[t][...], xs_ref[rows, columns]))

        by_suffix(clip_ref, start + out, 0, 2, body, None)


def second_kernel(clip_ref, part_ref, got_ref, mine_ref, before_ref, weight_ref, bias_ref, gain_ref, xs_ref, w0_ref, w1_ref, w2_ref, down_ref, edge_ref):
    width = got_ref.shape[2] // 2
    frames = part_ref.shape[0] - 2
    height = part_ref.shape[2] // width - 1
    outs = part_ref.shape[1]
    start = lax.axis_index("tm") * frames
    bias, gain = spread(bias_ref[...], width), spread(gain_ref[...], width)
    refs = (w0_ref, w1_ref, w2_ref)
    for t, ref in enumerate(refs):
        for i in range(3):
            ref[i * outs : (i + 1) * outs, :] = fold_taps(weight_ref, i, t, 2)
    for s in range(-2, frames):
        for h in range(-1, height):
            cols = pl.ds((h + 1) * width, width)
            if s < 0:
                act = before_ref[s + 2, :, cols].astype(F32)
            elif s >= frames - 2:
                act = mine_ref[s - frames + 2, :, cols].astype(F32)
            else:
                total = hidden_sum(part_ref, got_ref, s, h, width)
                if s < 2:
                    total = total + before_ref[2 + s, :, cols].astype(F32)
                act = act_rows(total, h, height, bias, gain)
            for j, tap in enumerate(column_taps(act)):
                xs_ref[pl.ds(((s + 2) * 3 + j) * outs, outs), cols] = tap

    def emit(out, y):
        y0, y1, y2 = (y[i * outs : (i + 1) * outs] for i in range(3))
        down_ref[out, :, :width] = y2[:, :width].astype(BF16)
        down_ref[out, :, width:] = (y1[:, :width] + y2[:, width:]).astype(BF16)
        edge_ref[out, :, :width] = y0[:, :width] + y1[:, width:]
        edge_ref[out, :, width:] = y0[:, width:]

    conv_second(xs_ref, refs, clip_ref, start, pl.ds(0, 2 * width), frames, emit)


def last_kernel(clip_ref, xs_ref, w0_ref, w1_ref, w2_ref, edge_ref, lat_ref, skip_ref, bias_ref, skip_bias_ref, out_ref):
    width = edge_ref.shape[2] // 2
    frames, outs, pixels = out_ref.shape
    height = pixels // width
    start = lax.axis_index("tm") * frames
    bias = spread(bias_ref[...] + skip_bias_ref[...], width)
    refs = (w0_ref, w1_ref, w2_ref)
    skip = skip_ref[...]

    def emit(out, y):
        y0, y1, y2 = (y[i * outs : (i + 1) * outs] for i in range(3))
        short = dot(skip, lat_ref[out])
        for r in range(height):
            total = short[:, r * width : (r + 1) * width] + bias
            for tap, row in ((y0, r - 1), (y1, r), (y2, r + 1)):
                if 1 <= row < height:
                    total = total + tap[:, (row - 1) * width : row * width]
            if r < 2:
                total = total + edge_ref[out, :, r * width : (r + 1) * width]
            out_ref[out, :, r * width : (r + 1) * width] = total

    conv_second(xs_ref, refs, clip_ref, start, pl.ds(2 * width, (height - 1) * width), frames, emit)


def call(kernel, shapes, operands, flops, smem=0):
    moved = sum(x.size * x.dtype.itemsize for x in operands) + sum(s.size * s.dtype.itemsize for s in shapes)
    single = len(shapes) == 1
    return pl.pallas_call(
        kernel,
        out_shape=shapes[0] if single else tuple(shapes),
        in_specs=[SMEM] * smem + [VMEM] * (len(operands) - smem),
        out_specs=VMEM if single else tuple(VMEM for _ in shapes),
        cost_estimate=pl.CostEstimate(flops=flops, bytes_accessed=moved, transcendentals=0),
        compiler_params=pltpu.CompilerParams(vmem_limit_bytes=20 << 20),
    )(*operands)


def moved_by(block, axis, distance):
    devices = range(lax.axis_size(axis))
    return lax.ppermute(block, axis, [(i, i + distance) for i in devices if i + distance in devices])


def shards(latent, clip_ids, gain_in, conv_in, bias_in, gain_mid, conv_mid, bias_mid, skip_weight, skip_bias):
    frames, chans, height, width = latent.shape
    outs = conv_in.shape[3]
    shape = jax.ShapeDtypeStruct
    lat = latent.reshape(frames, chans, height * width)
    row = lambda v: v.reshape(1, -1)
    deep, deep_mid, tall = 3 * chans, 3 * outs, 3 * outs
    work = 2 * tall * 3 * deep * frames * width
    xs, wt, wu, up, edge = call(
        first_kernel,
        [
            shape((frames * deep, height * width), BF16),
            shape((tall, 3 * deep), BF16),
            shape((tall, 2 * deep), BF16),
            shape((frames + 2, outs, 2 * width), BF16),
            shape((frames + 2, outs, 3 * width), F32),
        ],
        (clip_ids, lat, conv_in, row(gain_in)),
        work * 2,
        1,
    )
    got = moved_by(up, "rows", 1)
    part = call(
        inner_kernel,
        [shape((frames + 2, outs, (height + 1) * width), F32)],
        (clip_ids, xs, wt, wu, edge),
        work * (height - 2),
        1,
    )
    msg = call(
        later_kernel,
        [shape((4, outs, (height + 1) * width), BF16)],
        (part, got, row(bias_in), row(gain_mid)),
        1000,
    )
    before = moved_by(msg, "tm", 1)
    xs_mid, w0, w1, w2, down, edge_mid = call(
        second_kernel,
        [
            shape(((frames + 2) * deep_mid, (height + 1) * width), BF16),
            shape((tall, 3 * deep_mid), BF16),
            shape((tall, 2 * deep_mid), BF16),
            shape((tall, deep_mid), BF16),
            shape((frames, outs, 2 * width), BF16),
            shape((frames, outs, 2 * width), F32),
        ],
        (clip_ids, part, got, msg, before, conv_mid, row(bias_in), row(gain_mid)),
        work,
        1,
    )
    below = moved_by(down, "rows", -1)
    total = call(
        last_kernel,
        [shape((frames, outs, height * width), F32)],
        (clip_ids, xs_mid, w0, w1, w2, edge_mid, lat, skip_weight, row(bias_mid), row(skip_bias)),
        work * (height - 2) // 2,
        1,
    )
    tail = total[:, :, (height - 2) * width :] + below.astype(F32)
    result = jnp.concatenate([total[:, :, : (height - 2) * width], tail], axis=2)
    return result.astype(BF16).reshape(frames, outs, height, width)


def solution(mesh):
    return jax.shard_map(
        shards,
        mesh=mesh,
        in_specs=(P("tm", None, "rows", None), P(), P(), P(), P(), P(), P(), P(), P(), P()),
        out_specs=P("tm", None, "rows", None),
        check_vma=False,
    )
```

```python
import jax
import jax.numpy as jnp
from jax import lax
from jax.experimental import pallas as pl
from jax.experimental.pallas import tpu as pltpu
from jax.sharding import PartitionSpec as P

F32 = jnp.float32
BF16 = jnp.bfloat16
VMEM = pl.BlockSpec(memory_space=pltpu.VMEM)
SMEM = pl.BlockSpec(memory_space=pltpu.SMEM)
HBM = pl.BlockSpec(memory_space=pltpu.HBM)


def silu_norm(values, gain):
    mean_sq = jnp.mean(values * values, axis=0, keepdims=True)
    scaled = values * lax.rsqrt(mean_sq + 1e-06) * gain
    return scaled / (1.0 + jnp.exp(-scaled))


def column_taps(act):
    lane = lax.broadcasted_iota(jnp.int32, act.shape, 1)
    width = act.shape[1]
    left = jnp.where(lane == 0, 0.0, pltpu.roll(act, 1, 1))
    right = jnp.where(lane == width - 1, 0.0, pltpu.roll(act, width - 1, 1))
    return left.astype(BF16), act.astype(BF16), right.astype(BF16)


def spread(vector, width):
    return jnp.broadcast_to(vector, (width, vector.shape[1])).T


def kept(clip_ref, frame, back):
    final = clip_ref.shape[0] - 1
    here = clip_ref[jnp.clip(frame, 0, final)]
    there = clip_ref[jnp.clip(frame - back, 0, final)]
    return (frame - back >= 0) & (here == there)


def fold_taps(weight_ref, row_tap, first, last):
    return jnp.concatenate([weight_ref[t, row_tap, j] for t in range(first, last + 1) for j in range(3)], axis=1)


def dot(a, b):
    return jnp.dot(a, b, preferred_element_type=F32)


def by_suffix(clip_ref, frame, first, last, body, nothing):
    flags = [None if t == 2 else kept(clip_ref, frame, 2 - t) for t in range(first, last + 1)]
    prior = None
    for t, flag in zip(range(first, last + 1), flags):
        here = flag if prior is None else (~prior if flag is None else ~prior & flag)
        if here is None:
            body(t)
            return
        pl.when(here)(lambda t=t: body(t))
        prior = flag
    if last != 2:
        pl.when(~prior)(nothing)


def norm_frame(lat_ref, frame, rows, gain, xs_ref):
    _, chans, height, width = lat_ref.shape
    values = lat_ref[frame].reshape(chans, height * width)
    for n, r in enumerate(rows):
        act = silu_norm(values[:, r * width : (r + 1) * width].astype(F32), gain)
        for j, tap in enumerate(column_taps(act)):
            xs_ref[pl.ds((frame * 3 + j) * chans, chans), n * width : (n + 1) * width] = tap


def conv_first(xs_ref, wt_ref, wu_ref, clip_ref, start, frames, emit):
    depth = xs_ref.shape[0] // frames
    for out in range(frames + 2):
        first, last = max(0, 2 - out), min(2, frames + 1 - out)

        def body(t, out=out, last=last):
            rows = pl.ds((out - 2 + t) * depth, (last + 1 - t) * depth)
            if t == 1:
                weight = wu_ref[:, : (last + 1 - t) * depth]
            else:
                weight = wt_ref[:, t * depth : (last + 1) * depth]
            emit(out, dot(weight, xs_ref[rows, :]))

        def nothing(out=out):
            emit(out, jnp.zeros((wt_ref.shape[0], xs_ref.shape[1]), F32))

        by_suffix(clip_ref, start + out, first, last, body, nothing)


def first_kernel(clip_hbm, lat_hbm, weight_hbm, gain_hbm, wt_ref, wu_ref, up_ref, edge_ref, lat_ref, xs_ref, weight_ref, gain_ref, clip_ref, sems):
    frames, chans, height, width = lat_ref.shape
    outs = weight_ref.shape[3]
    start = lax.axis_index("tm") * frames
    pairs = [(gain_hbm, gain_ref)] + [(lat_hbm.at[f], lat_ref.at[f]) for f in range(frames)]
    pairs += [(clip_hbm, clip_ref), (weight_hbm, weight_ref)]
    copies = [pltpu.make_async_copy(a, b, sems.at[n]) for n, (a, b) in enumerate(pairs)]
    for copy in copies:
        copy.start()
    copies[0].wait()
    gain = spread(gain_ref[...], width)
    for f in range(frames):
        copies[1 + f].wait()
        norm_frame(lat_ref, f, (height - 2, height - 1), gain, xs_ref)
    for copy in copies[1 + frames :]:
        copy.wait()
    for i in range(3):
        wt_ref[i * outs : (i + 1) * outs, :] = fold_taps(weight_ref, i, 0, 2)
        wu_ref[i * outs : (i + 1) * outs, :] = fold_taps(weight_ref, i, 1, 2)

    def emit(out, y):
        y0, y1, y2 = (y[i * outs : (i + 1) * outs] for i in range(3))
        far = y0[:, :width] + y1[:, width:]
        up_ref[out, :, :width] = far.astype(BF16)
        up_ref[out, :, width:] = y0[:, width:].astype(BF16)
        edge_ref[out, :, :width] = y2[:, :width]
        edge_ref[out, :, width : 2 * width] = y1[:, :width] + y2[:, width:]
        edge_ref[out, :, 2 * width :] = far

    conv_first(xs_ref, wt_ref, wu_ref, clip_ref, start, frames, emit)


def inner_kernel(clip_ref, lat_ref, gain_ref, wt_ref, wu_ref, edge_ref, bias_ref, gain_mid_ref, part_ref, early_ref, xs_ref):
    frames, chans, height, width = lat_ref.shape
    outs = edge_ref.shape[1]
    inner = height - 2
    start = lax.axis_index("tm") * frames
    gain = spread(gain_ref[...], width)
    bias, gain_mid = spread(bias_ref[...], width), spread(gain_mid_ref[...], width)
    for f in range(frames):
        norm_frame(lat_ref, f, range(inner), gain, xs_ref)

    def emit(out, y):
        y0, y1, y2 = (y[i * outs : (i + 1) * outs] for i in range(3))
        for h in range(-1, inner + 2):
            total = None
            for tap, row in ((y0, h - 1), (y1, h), (y2, h + 1)):
                if 0 <= row < inner:
                    term = tap[:, row * width : (row + 1) * width]
                    total = term if total is None else total + term
            if h >= inner - 1:
                e = h - inner + 1
                term = edge_ref[out, :, e * width : (e + 1) * width]
                total = term if total is None else total + term
            part_ref[out, :, (h + 1) * width : (h + 2) * width] = total

    conv_first(xs_ref, wt_ref, wu_ref, clip_ref, start, frames, emit)
    for k in range(4):
        for h in range(1, height):
            total = part_ref[frames - 2 + k, :, (h + 1) * width : (h + 2) * width]
            if k < 2:
                total = act_rows(total, h, height, bias, gain_mid)
            early_ref[k, :, (h - 1) * width : h * width] = total.astype(BF16)


def act_rows(total, h, height, bias, gain):
    hidden = (total + bias).astype(BF16).astype(F32)
    act = silu_norm(hidden, gain)
    if h == -1:
        return jnp.where(lax.axis_index("rows") > 0, act, 0.0)
    if h == height - 1:
        return jnp.where(lax.axis_index("rows") == lax.axis_size("rows") - 1, act, 0.0)
    return act


def hidden_sum(part_ref, got_ref, out, h, width):
    total = part_ref[out, :, (h + 1) * width : (h + 2) * width]
    if h < 1:
        total = total + got_ref[out, :, (h + 1) * width : (h + 2) * width].astype(F32)
    return total


def late_kernel(part_ref, got_ref, bias_ref, gain_ref, late_ref):
    width = got_ref.shape[2] // 2
    frames = part_ref.shape[0] - 2
    height = part_ref.shape[2] // width - 1
    bias, gain = spread(bias_ref[...], width), spread(gain_ref[...], width)
    for k in range(4):
        for h in (-1, 0):
            total = hidden_sum(part_ref, got_ref, frames - 2 + k, h, width)
            if k < 2:
                total = act_rows(total, h, height, bias, gain)
            late_ref[k, :, (h + 1) * width : (h + 2) * width] = total.astype(BF16)


def conv_second(xs_ref, wt_refs, clip_ref, start, frames, emit):
    depth = xs_ref.shape[0] // (frames + 2)
    for out in range(frames):

        def body(t, out=out):
            rows = pl.ds((out + t) * depth, (3 - t) * depth)
            emit(out, dot(wt_refs[t][...], xs_ref[rows, :]))

        by_suffix(clip_ref, start + out, 0, 2, body, None)


def act_taps(mine_ref, before_ref, sums, rows, height, bias, gain, frames, xs_ref):
    outs = mine_ref.shape[1]
    width = mine_ref.shape[2] // len(rows)
    for s in range(-2, frames):
        for n, h in enumerate(rows):
            cols = pl.ds(n * width, width)
            if s < 0:
                act = before_ref[s + 2, :, cols].astype(F32)
            elif s >= frames - 2:
                act = mine_ref[s - frames + 2, :, cols].astype(F32)
            else:
                total = sums(s, h)
                if s < 2:
                    total = total + before_ref[2 + s, :, cols].astype(F32)
                act = act_rows(total, h, height, bias, gain)
            for j, tap in enumerate(column_taps(act)):
                xs_ref[pl.ds(((s + 2) * 3 + j) * outs, outs), cols] = tap


def body_kernel(clip_ref, part_ref, mine_ref, before_ref, weight_ref, bias_ref, gain_ref, lat_ref, skip_ref, bias_mid_ref, skip_bias_ref, w0_ref, w1_ref, w2_ref, total_ref, xs_ref):
    frames, chans, height, width = lat_ref.shape
    outs = part_ref.shape[1]
    start = lax.axis_index("tm") * frames
    bias, gain = spread(bias_ref[...], width), spread(gain_ref[...], width)
    shift = spread(bias_mid_ref[...] + skip_bias_ref[...], width)
    refs = (w0_ref, w1_ref, w2_ref)
    for t, ref in enumerate(refs):
        for i in range(3):
            ref[i * outs : (i + 1) * outs, :] = fold_taps(weight_ref, i, t, 2)
    sums = lambda s, h: part_ref[s, :, (h + 1) * width : (h + 2) * width]
    act_taps(mine_ref, before_ref, sums, range(1, height), height, bias, gain, frames, xs_ref)
    skip = skip_ref[...]

    def emit(out, y):
        y0, y1, y2 = (y[i * outs : (i + 1) * outs] for i in range(3))
        short = dot(skip, lat_ref[out].reshape(chans, height * width))
        for r in range(height):
            total = short[:, r * width : (r + 1) * width] + shift
            for tap, row in ((y0, r - 1), (y1, r), (y2, r + 1)):
                if 1 <= row < height:
                    total = total + tap[:, (row - 1) * width : row * width]
            total_ref[out, :, r * width : (r + 1) * width] = total

    conv_second(xs_ref, refs, clip_ref, start, frames, emit)


def edge_kernel(clip_ref, part_ref, got_ref, mine_ref, before_ref, bias_ref, gain_ref, w0_ref, w1_ref, w2_ref, down_ref, edge_ref, xs_ref):
    width = got_ref.shape[2] // 2
    frames = part_ref.shape[0] - 2
    height = part_ref.shape[2] // width - 1
    outs = part_ref.shape[1]
    start = lax.axis_index("tm") * frames
    bias, gain = spread(bias_ref[...], width), spread(gain_ref[...], width)
    sums = lambda s, h: hidden_sum(part_ref, got_ref, s, h, width)
    act_taps(mine_ref, before_ref, sums, (-1, 0), height, bias, gain, frames, xs_ref)

    def emit(out, y):
        y0, y1, y2 = (y[i * outs : (i + 1) * outs] for i in range(3))
        down_ref[out, :, :width] = y2[:, :width].astype(BF16)
        down_ref[out, :, width:] = (y1[:, :width] + y2[:, width:]).astype(BF16)
        edge_ref[out, :, :width] = y0[:, :width] + y1[:, width:]
        edge_ref[out, :, width:] = y0[:, width:]

    conv_second(xs_ref, (w0_ref, w1_ref, w2_ref), clip_ref, start, frames, emit)


def last_kernel(total_ref, edge_ref, below_ref, out_ref):
    frames, outs, height, width = out_ref.shape
    for f in range(frames):
        rows = [total_ref[f, :, r * width : (r + 1) * width] for r in range(height)]
        for n in range(2):
            cols = pl.ds(n * width, width)
            rows[n] = rows[n] + edge_ref[f, :, cols]
            rows[height - 2 + n] = rows[height - 2 + n] + below_ref[f, :, cols].astype(F32)
        out_ref[f] = jnp.concatenate(rows, axis=1).reshape(outs, height, width).astype(BF16)


def call(kernel, shapes, operands, flops, places=(), scratch=()):
    moved = sum(x.size * x.dtype.itemsize for x in operands) + sum(s.size * s.dtype.itemsize for s in shapes)
    single = len(shapes) == 1
    places = list(places) + [VMEM] * (len(operands) - len(places))
    return pl.pallas_call(
        kernel,
        out_shape=shapes[0] if single else tuple(shapes),
        in_specs=places,
        out_specs=VMEM if single else tuple(VMEM for _ in shapes),
        scratch_shapes=list(scratch),
        cost_estimate=pl.CostEstimate(flops=flops, bytes_accessed=moved, transcendentals=0),
        compiler_params=pltpu.CompilerParams(vmem_limit_bytes=20 << 20),
    )(*operands)


def moved_by(block, axis, distance):
    devices = range(lax.axis_size(axis))
    return lax.ppermute(block, axis, [(i, i + distance) for i in devices if i + distance in devices])


def shards(latent, clip_ids, gain_in, conv_in, bias_in, gain_mid, conv_mid, bias_mid, skip_weight, skip_bias):
    frames, chans, height, width = latent.shape
    outs = conv_in.shape[3]
    shape = jax.ShapeDtypeStruct
    row = lambda v: v.reshape(1, -1)
    deep, deep_mid, tall = 3 * chans, 3 * outs, 3 * outs
    work = 2 * tall * 3 * deep * frames * width
    wt, wu, up, edge, lat = call(
        first_kernel,
        [
            shape((tall, 3 * deep), BF16),
            shape((tall, 2 * deep), BF16),
            shape((frames + 2, outs, 2 * width), BF16),
            shape((frames + 2, outs, 3 * width), F32),
            shape(latent.shape, BF16),
        ],
        tuple(pltpu.with_memory_space_constraint(x, pltpu.HBM) for x in (clip_ids, latent, conv_in, row(gain_in))),
        work * 2,
        [HBM] * 4,
        [
            pltpu.VMEM((frames * deep, 2 * width), BF16),
            pltpu.VMEM(conv_in.shape, BF16),
            pltpu.VMEM((1, chans), F32),
            pltpu.SMEM(clip_ids.shape, jnp.int32),
            pltpu.SemaphoreType.DMA((frames + 3,)),
        ],
    )
    got = moved_by(up, "rows", 1)
    part, early = call(
        inner_kernel,
        [shape((frames + 2, outs, (height + 1) * width), F32), shape((4, outs, (height - 1) * width), BF16)],
        (clip_ids, lat, row(gain_in), wt, wu, edge, row(bias_in), row(gain_mid)),
        work * (height - 2),
        [SMEM],
        [pltpu.VMEM((frames * deep, (height - 2) * width), BF16)],
    )
    before_early = moved_by(early, "tm", 1)
    late = call(
        late_kernel,
        [shape((4, outs, 2 * width), BF16)],
        (part, got, row(bias_in), row(gain_mid)),
        1000,
    )
    before_late = moved_by(late, "tm", 1)
    w0, w1, w2, total = call(
        body_kernel,
        [
            shape((tall, 3 * deep_mid), BF16),
            shape((tall, 2 * deep_mid), BF16),
            shape((tall, deep_mid), BF16),
            shape((frames, outs, height * width), F32),
        ],
        (clip_ids, part, early, before_early, conv_mid, row(bias_in), row(gain_mid), lat, skip_weight, row(bias_mid), row(skip_bias)),
        work * (height - 1) // 2,
        [SMEM],
        [pltpu.VMEM(((frames + 2) * deep_mid, (height - 1) * width), BF16)],
    )
    down, edge_mid = call(
        edge_kernel,
        [shape((frames, outs, 2 * width), BF16), shape((frames, outs, 2 * width), F32)],
        (clip_ids, part, got, late, before_late, row(bias_in), row(gain_mid), w0, w1, w2),
        work,
        [SMEM],
        [pltpu.VMEM(((frames + 2) * deep_mid, 2 * width), BF16)],
    )
    below = moved_by(down, "rows", -1)
    return call(last_kernel, [shape((frames, outs, height, width), BF16)], (total, edge_mid, below), 1000)


def solution(mesh):
    return jax.shard_map(
        shards,
        mesh=mesh,
        in_specs=(P("tm", None, "rows", None), P(), P(), P(), P(), P(), P(), P(), P(), P()),
        out_specs=P("tm", None, "rows", None),
        check_vma=False,
    )
```

```python
import jax
import jax.numpy as jnp
from jax import lax
from jax.experimental import pallas as pl
from jax.experimental.pallas import tpu as pltpu
from jax.sharding import PartitionSpec as P


F32 = jnp.float32
BF16 = jnp.bfloat16
VMEM = pl.BlockSpec(memory_space=pltpu.VMEM)
SMEM = pl.BlockSpec(memory_space=pltpu.SMEM)
HBM = pl.BlockSpec(memory_space=pltpu.HBM)


def silu_norm(values, gain):
    mean_sq = jnp.mean(values * values, axis=0, keepdims=True)
    scaled = values * lax.rsqrt(mean_sq + 1e-06) * gain
    return scaled / (1.0 + jnp.exp(-scaled))


def column_taps(act):
    lane = lax.broadcasted_iota(jnp.int32, act.shape, 1)
    width = act.shape[1]
    left = jnp.where(lane == 0, 0.0, pltpu.roll(act, 1, 1))
    right = jnp.where(lane == width - 1, 0.0, pltpu.roll(act, width - 1, 1))
    return left.astype(BF16), act.astype(BF16), right.astype(BF16)


def spread(vector, width):
    return jnp.broadcast_to(vector, (width, vector.shape[1])).T


def kept(clip_ref, frame, back):
    final = clip_ref.shape[0] - 1
    here = clip_ref[jnp.clip(frame, 0, final)]
    there = clip_ref[jnp.clip(frame - back, 0, final)]
    return (frame - back >= 0) & (here == there)


def fold_taps(weight_ref, row_tap):
    return jnp.concatenate([weight_ref[t, row_tap, j] for t in range(3) for j in range(3)], axis=1)


def dot(a, b):
    return jnp.dot(a, b, preferred_element_type=F32)


def norm_frame(lat_ref, frame, rows, gain, xs_ref):
    _, chans, height, width = lat_ref.shape
    values = lat_ref[frame].reshape(chans, height * width)
    for n, r in enumerate(rows):
        act = silu_norm(values[:, r * width : (r + 1) * width].astype(F32), gain)
        for j, tap in enumerate(column_taps(act)):
            xs_ref[pl.ds((frame * 3 + j) * chans, chans), n * width : (n + 1) * width] = tap


def clear_last(xs_ref, depth):
    xs_ref[pl.ds(xs_ref.shape[0] - depth, depth), :] = jnp.zeros((depth, xs_ref.shape[1]), xs_ref.dtype)


def conv_frame(xs_ref, wt_ref, clip_ref, start, out, lag):
    depth = wt_ref.shape[1] // 3
    zero = xs_ref.shape[0] // depth - 1
    taps = [t for t in range(3) if 0 <= out - 2 + t + lag < zero]
    blocks = []
    for t in taps:
        block = out - 2 + t + lag
        if t < 2:
            block = jnp.where(kept(clip_ref, start + out, 2 - t), block, zero)
        blocks.append(xs_ref[pl.ds(pl.multiple_of(block * depth, depth), depth), :])
    first = taps[0] * depth
    spare = first % 128
    if spare:
        blocks.insert(0, xs_ref[pl.ds(zero * depth, spare), :])
    weight = wt_ref[:, first - spare : (taps[-1] + 1) * depth]
    outs = weight.shape[0] // 3
    y = dot(weight, blocks[0] if len(blocks) == 1 else jnp.concatenate(blocks, axis=0))
    return [y[i * outs : (i + 1) * outs] for i in range(3)]


def first_kernel(clip_hbm, lat_hbm, weight_hbm, gain_hbm, wt_ref, up_ref, edge_ref, lat_ref, xs_ref, weight_ref, gain_ref, clip_ref, sems):
    frames, chans, height, width = lat_ref.shape
    outs = weight_ref.shape[3]
    start = lax.axis_index("tm") * frames
    pairs = [(gain_hbm, gain_ref)] + [(lat_hbm.at[f], lat_ref.at[f]) for f in range(frames)]
    pairs += [(clip_hbm, clip_ref), (weight_hbm, weight_ref)]
    copies = [pltpu.make_async_copy(a, b, sems.at[n]) for n, (a, b) in enumerate(pairs)]
    for copy in copies:
        copy.start()
    clear_last(xs_ref, 3 * chans)
    copies[0].wait()
    gain = spread(gain_ref[...], width)
    for f in range(frames):
        copies[1 + f].wait()
        norm_frame(lat_ref, f, (height - 2, height - 1), gain, xs_ref)
    for copy in copies[1 + frames :]:
        copy.wait()
    for i in range(3):
        wt_ref[i * outs : (i + 1) * outs, :] = fold_taps(weight_ref, i)
    for out in range(frames + 2):
        y0, y1, y2 = conv_frame(xs_ref, wt_ref, clip_ref, start, out, 0)
        far = y0[:, :width] + y1[:, width:]
        up_ref[out, :, :width] = far.astype(BF16)
        up_ref[out, :, width:] = y0[:, width:].astype(BF16)
        edge_ref[out, :, :width] = y2[:, :width]
        edge_ref[out, :, width : 2 * width] = y1[:, :width] + y2[:, width:]
        edge_ref[out, :, 2 * width :] = far


def inner_rows(xs_ref, wt_ref, clip_ref, start, edge_ref, out, width):
    inner = xs_ref.shape[1] // width
    y0, y1, y2 = conv_frame(xs_ref, wt_ref, clip_ref, start, out, 0)
    rows = []
    for h in range(-1, inner + 2):
        total = None
        for tap, row in ((y0, h - 1), (y1, h), (y2, h + 1)):
            if 0 <= row < inner:
                term = tap[:, row * width : (row + 1) * width]
                total = term if total is None else total + term
        if h >= inner - 1:
            e = h - inner + 1
            term = edge_ref[out, :, e * width : (e + 1) * width]
            total = term if total is None else total + term
        rows.append(total)
    return rows


def inner_kernel(clip_ref, lat_ref, gain_ref, wt_ref, edge_ref, bias_ref, gain_mid_ref, part_ref, early_ref, xs_ref):
    frames, chans, height, width = lat_ref.shape
    start = lax.axis_index("tm") * frames
    gain = spread(gain_ref[...], width)
    bias, gain_mid = spread(bias_ref[...], width), spread(gain_mid_ref[...], width)
    clear_last(xs_ref, 3 * chans)
    for f in range(frames):
        norm_frame(lat_ref, f, range(height - 2), gain, xs_ref)
    for k in range(4):
        rows = inner_rows(xs_ref, wt_ref, clip_ref, start, edge_ref, frames - 2 + k, width)
        for h, total in enumerate(rows, -1):
            if h < 1:
                part_ref[k, :, (h + 1) * width : (h + 2) * width] = total
            else:
                if k < 2:
                    total = act_rows(total, h, height, bias, gain_mid)
                early_ref[k, :, (h - 1) * width : h * width] = total.astype(BF16)


def head_kernel(clip_ref, xs_ref, wt_ref, edge_ref, weight_ref, head_ref, w_ref):
    frames, outs, _ = head_ref.shape
    width = edge_ref.shape[2] // 3
    start = lax.axis_index("tm") * (edge_ref.shape[0] - 2)
    for i in range(3):
        w_ref[i * outs : (i + 1) * outs, :] = fold_taps(weight_ref, i)
    for out in range(frames):
        rows = inner_rows(xs_ref, wt_ref, clip_ref, start, edge_ref, out, width)
        for n, total in enumerate(rows):
            head_ref[out, :, n * width : (n + 1) * width] = total


def act_rows(total, h, height, bias, gain):
    hidden = (total + bias).astype(BF16).astype(F32)
    act = silu_norm(hidden, gain)
    if h == -1:
        return jnp.where(lax.axis_index("rows") > 0, act, 0.0)
    if h == height - 1:
        return jnp.where(lax.axis_index("rows") == lax.axis_size("rows") - 1, act, 0.0)
    return act


def late_kernel(part_ref, got_ref, bias_ref, gain_ref, late_ref):
    width = got_ref.shape[2] // 2
    frames = got_ref.shape[0] - 2
    bias, gain = spread(bias_ref[...], width), spread(gain_ref[...], width)
    for k in range(4):
        for h in (-1, 0):
            cols = pl.ds((h + 1) * width, width)
            total = part_ref[k, :, cols] + got_ref[frames - 2 + k, :, cols].astype(F32)
            if k < 2:
                total = act_rows(total, h, 0, bias, gain)
            late_ref[k, :, cols] = total.astype(BF16)


def act_taps(mine_ref, before_ref, sums, rows, height, bias, gain, frames, xs_ref):
    outs = mine_ref.shape[1]
    width = mine_ref.shape[2] // len(rows)
    for s in range(-2, frames):
        for n, h in enumerate(rows):
            cols = pl.ds(n * width, width)
            if s < 0:
                act = before_ref[s + 2, :, cols].astype(F32)
            elif s >= frames - 2:
                act = mine_ref[s - frames + 2, :, cols].astype(F32)
            else:
                total = sums(s, h)
                if s < 2:
                    total = total + before_ref[2 + s, :, cols].astype(F32)
                act = act_rows(total, h, height, bias, gain)
            for j, tap in enumerate(column_taps(act)):
                xs_ref[pl.ds(((s + 2) * 3 + j) * outs, outs), cols] = tap


def edge_kernel(clip_ref, head_ref, got_ref, mine_ref, before_ref, bias_ref, gain_ref, w_ref, down_ref, edge_ref, xs_ref):
    width = got_ref.shape[2] // 2
    frames = got_ref.shape[0] - 2
    start = lax.axis_index("tm") * frames
    bias, gain = spread(bias_ref[...], width), spread(gain_ref[...], width)

    def sums(s, h):
        cols = pl.ds((h + 1) * width, width)
        return head_ref[s, :, cols] + got_ref[s, :, cols].astype(F32)

    clear_last(xs_ref, w_ref.shape[0])
    act_taps(mine_ref, before_ref, sums, (-1, 0), 0, bias, gain, frames, xs_ref)
    for out in range(frames):
        y0, y1, y2 = conv_frame(xs_ref, w_ref, clip_ref, start, out, 2)
        down_ref[out, :, :width] = y2[:, :width].astype(BF16)
        down_ref[out, :, width:] = (y1[:, :width] + y2[:, width:]).astype(BF16)
        edge_ref[out, :, :width] = y0[:, :width] + y1[:, width:]
        edge_ref[out, :, width:] = y0[:, width:]


def body_kernel(clip_ref, head_ref, mine_ref, before_ref, w_ref, edge_ref, bias_ref, gain_ref, lat_ref, skip_ref, bias_mid_ref, skip_bias_ref, total_ref, xs_ref):
    frames, chans, height, width = lat_ref.shape
    start = lax.axis_index("tm") * frames
    bias, gain = spread(bias_ref[...], width), spread(gain_ref[...], width)
    shift = spread(bias_mid_ref[...] + skip_bias_ref[...], width)
    sums = lambda s, h: head_ref[s, :, (h + 1) * width : (h + 2) * width]
    clear_last(xs_ref, w_ref.shape[0])
    act_taps(mine_ref, before_ref, sums, range(1, height), height, bias, gain, frames, xs_ref)
    skip = skip_ref[...]
    for out in range(frames):
        y0, y1, y2 = conv_frame(xs_ref, w_ref, clip_ref, start, out, 2)
        short = dot(skip, lat_ref[out].reshape(chans, height * width))
        for r in range(height):
            cols = pl.ds(r * width, width)
            total = short[:, r * width : (r + 1) * width] + shift
            for tap, row in ((y0, r - 1), (y1, r), (y2, r + 1)):
                if 1 <= row < height:
                    total = total + tap[:, (row - 1) * width : row * width]
            if r < 2:
                total = total + edge_ref[out, :, cols]
            total_ref[out, :, cols] = total


def last_kernel(total_ref, below_ref, out_ref):
    frames, outs, height, width = out_ref.shape
    for f in range(frames):
        rows = [total_ref[f, :, r * width : (r + 1) * width] for r in range(height)]
        for n in range(2):
            rows[height - 2 + n] = rows[height - 2 + n] + below_ref[f, :, n * width : (n + 1) * width].astype(F32)
        out_ref[f] = jnp.concatenate(rows, axis=1).reshape(outs, height, width).astype(BF16)


def call(kernel, shapes, operands, flops, places=(), scratch=()):
    moved = sum(x.size * x.dtype.itemsize for x in operands) + sum(s.size * s.dtype.itemsize for s in shapes)
    single = len(shapes) == 1
    places = list(places) + [VMEM] * (len(operands) - len(places))
    return pl.pallas_call(
        kernel,
        out_shape=shapes[0] if single else tuple(shapes),
        in_specs=places,
        out_specs=VMEM if single else tuple(VMEM for _ in shapes),
        scratch_shapes=list(scratch),
        cost_estimate=pl.CostEstimate(flops=flops, bytes_accessed=moved, transcendentals=0),
        compiler_params=pltpu.CompilerParams(vmem_limit_bytes=20 << 20),
    )(*operands)


def moved_by(block, axis, distance):
    devices = range(lax.axis_size(axis))
    return lax.ppermute(block, axis, [(i, i + distance) for i in devices if i + distance in devices])


def shards(latent, clip_ids, gain_in, conv_in, bias_in, gain_mid, conv_mid, bias_mid, skip_weight, skip_bias):
    frames, chans, height, width = latent.shape
    outs = conv_in.shape[3]
    shape = jax.ShapeDtypeStruct
    row = lambda v: v.reshape(1, -1)
    deep, deep_mid, tall = 3 * chans, 3 * outs, 3 * outs
    work = 2 * tall * 3 * deep * frames * width
    wt, up, edge, lat = call(
        first_kernel,
        [
            shape((tall, 3 * deep), BF16),
            shape((frames + 2, outs, 2 * width), BF16),
            shape((frames + 2, outs, 3 * width), F32),
            shape(latent.shape, BF16),
        ],
        tuple(pltpu.with_memory_space_constraint(x, pltpu.HBM) for x in (clip_ids, latent, conv_in, row(gain_in))),
        work * 2,
        [HBM] * 4,
        [
            pltpu.VMEM(((frames + 1) * deep, 2 * width), BF16),
            pltpu.VMEM(conv_in.shape, BF16),
            pltpu.VMEM((1, chans), F32),
            pltpu.SMEM(clip_ids.shape, jnp.int32),
            pltpu.SemaphoreType.DMA((frames + 3,)),
        ],
    )
    got = moved_by(up, "rows", 1)
    part, early, xs = call(
        inner_kernel,
        [
            shape((4, outs, 2 * width), F32),
            shape((4, outs, (height - 1) * width), BF16),
            shape(((frames + 1) * deep, (height - 2) * width), BF16),
        ],
        (clip_ids, lat, row(gain_in), wt, edge, row(bias_in), row(gain_mid)),
        work * (height - 2),
        [SMEM],
    )
    before_early = moved_by(early, "tm", 1)
    head, w_mid = call(
        head_kernel,
        [shape((frames - 2, outs, (height + 1) * width), F32), shape((tall, 3 * deep_mid), BF16)],
        (clip_ids, xs, wt, edge, conv_mid),
        work,
        [SMEM],
    )
    late = call(
        late_kernel,
        [shape((4, outs, 2 * width), BF16)],
        (part, got, row(bias_in), row(gain_mid)),
        1000,
    )
    before_late = moved_by(late, "tm", 1)
    down, edge_mid = call(
        edge_kernel,
        [shape((frames, outs, 2 * width), BF16), shape((frames, outs, 2 * width), F32)],
        (clip_ids, head, got, late, before_late, row(bias_in), row(gain_mid), w_mid),
        work,
        [SMEM],
        [pltpu.VMEM(((frames + 3) * deep_mid, 2 * width), BF16)],
    )
    below = moved_by(down, "rows", -1)
    total = call(
        body_kernel,
        [shape((frames, outs, height * width), F32)],
        (clip_ids, head, early, before_early, w_mid, edge_mid, row(bias_in), row(gain_mid), lat, skip_weight, row(bias_mid), row(skip_bias)),
        work * (height - 1) // 2,
        [SMEM],
        [pltpu.VMEM(((frames + 3) * deep_mid, (height - 1) * width), BF16)],
    )
    return call(last_kernel, [shape((frames, outs, height, width), BF16)], (total, below), 1000)


def solution(mesh):
    return jax.shard_map(
        shards,
        mesh=mesh,
        in_specs=(P("tm", None, "rows", None), P(), P(), P(), P(), P(), P(), P(), P(), P()),
        out_specs=P("tm", None, "rows", None),
        check_vma=False,
    )
```

```python
import jax
import jax.numpy as jnp
from jax import lax
from jax.experimental import pallas as pl
from jax.experimental.pallas import tpu as pltpu
from jax.sharding import PartitionSpec as P


F32 = jnp.float32
BF16 = jnp.bfloat16
VMEM = pl.BlockSpec(memory_space=pltpu.VMEM)
HBM = pl.BlockSpec(memory_space=pltpu.HBM)


def silu_norm(values, gain):
    mean_sq = jnp.mean(values * values, axis=0, keepdims=True)
    scaled = values * lax.rsqrt(mean_sq + 1e-06) * gain
    return scaled / (1.0 + jnp.exp(-scaled))


def column_taps(act):
    lane = lax.broadcasted_iota(jnp.int32, act.shape, 1)
    width = act.shape[1]
    left = jnp.where(lane == 0, 0.0, pltpu.roll(act, 1, 1))
    right = jnp.where(lane == width - 1, 0.0, pltpu.roll(act, width - 1, 1))
    return left.astype(BF16), act.astype(BF16), right.astype(BF16)


def spread(vector, width):
    return jnp.broadcast_to(vector, (width, vector.shape[1])).T


def kept(clip_ref, frame, back):
    final = clip_ref.shape[0] - 1
    here = clip_ref[jnp.clip(frame, 0, final)]
    there = clip_ref[jnp.clip(frame - back, 0, final)]
    return (frame - back >= 0) & (here == there)


def fold_taps(weight_ref, row_tap, taps):
    return jnp.concatenate([weight_ref[t, row_tap, j] for t in taps for j in range(3)], axis=1)


def dot(a, b):
    return jnp.dot(a, b, preferred_element_type=F32)


def norm_frame(lat_ref, frame, rows, gain, xs_ref):
    _, chans, height, width = lat_ref.shape
    values = lat_ref[frame].reshape(chans, height * width)
    for n, r in enumerate(rows):
        act = silu_norm(values[:, r * width : (r + 1) * width].astype(F32), gain)
        for j, tap in enumerate(column_taps(act)):
            xs_ref[pl.ds((frame * 3 + j) * chans, chans), n * width : (n + 1) * width] = tap


def conv_frame(xs_ref, wt_ref, keep_ref, out, lag):
    depth = wt_ref.shape[1] // 3
    columns = xs_ref.shape[1]
    taps = [t for t in range(3) if 0 <= out - 2 + t + lag < xs_ref.shape[0] // depth]
    blocks = []
    for t in taps:
        block = xs_ref[pl.ds((out - 2 + t + lag) * depth, depth), :]
        if t < 2:
            keep = keep_ref[2 * out + 1 - t]
            high, width = keep.shape
            keep = jnp.concatenate([keep] * (columns // width), axis=1)
            block = (block.reshape(depth // high, high, columns) * keep[None]).reshape(depth, columns)
        blocks.append(block)
    first = taps[0] * depth
    spare = first % 128
    if spare:
        blocks.insert(0, jnp.zeros((spare, columns), BF16))
    weight = wt_ref[:, first - spare : (taps[-1] + 1) * depth]
    outs = weight.shape[0] // 3
    y = dot(weight, blocks[0] if len(blocks) == 1 else jnp.concatenate(blocks, axis=0))
    return [y[i * outs : (i + 1) * outs] for i in range(3)]


def first_kernel(clip_hbm, lat_hbm, weight_hbm, gain_hbm, wt_ref, up_ref, edge_ref, lat_ref, keep_ref, xs_ref, weight_ref, gain_ref, clip_ref, sems):
    frames, _, height, width = lat_ref.shape
    outs = weight_ref.shape[3]
    start = lax.axis_index("tm") * frames
    pairs = [(gain_hbm, gain_ref)] + [(lat_hbm.at[f], lat_ref.at[f]) for f in range(frames)] + [(clip_hbm, clip_ref)]
    pairs += [(weight_hbm, weight_ref)]
    copies = [pltpu.make_async_copy(a, b, sems.at[n]) for n, (a, b) in enumerate(pairs)]
    for copy in copies:
        copy.start()
    copies[0].wait()
    gain = spread(gain_ref[...], width)
    for f in range(frames):
        copies[1 + f].wait()
        norm_frame(lat_ref, f, (height - 2, height - 1), gain, xs_ref)
    copies[1 + frames].wait()
    for out in range(frames + 2):
        for back in (1, 2):
            flag = jnp.where(kept(clip_ref, start + out, back), 1.0, 0.0)
            keep_ref[2 * out + back - 1] = jnp.full(keep_ref.shape[1:], flag, F32).astype(BF16)

    def message(out):
        y0, y1, y2 = conv_frame(xs_ref, wt_ref, keep_ref, out, 0)
        far = y0[:, :width] + y1[:, width:]
        up_ref[out, :, :width] = far.astype(BF16)
        up_ref[out, :, width:] = y0[:, width:].astype(BF16)
        edge_ref[out, :, :width] = y2[:, :width]
        edge_ref[out, :, width : 2 * width] = y1[:, :width] + y2[:, width:]
        edge_ref[out, :, 2 * width :] = far

    for copy in copies[2 + frames :]:
        copy.wait()
    for i in range(3):
        wt_ref[i * outs : (i + 1) * outs, :] = fold_taps(weight_ref, i, range(3))
    for out in range(frames + 2):
        message(out)


def inner_rows(xs_ref, wt_ref, keep_ref, edge_ref, out, width):
    inner = xs_ref.shape[1] // width
    y0, y1, y2 = conv_frame(xs_ref, wt_ref, keep_ref, out, 0)
    rows = []
    for h in range(-1, inner + 2):
        total = None
        for tap, row in ((y0, h - 1), (y1, h), (y2, h + 1)):
            if 0 <= row < inner:
                term = tap[:, row * width : (row + 1) * width]
                total = term if total is None else total + term
        if h >= inner - 1:
            e = h - inner + 1
            term = edge_ref[out, :, e * width : (e + 1) * width]
            total = term if total is None else total + term
        rows.append(total)
    return rows


def inner_kernel(keep_ref, lat_ref, gain_ref, wt_ref, edge_ref, bias_ref, gain_mid_ref, part_ref, early_ref, xs_ref, mid_ref):
    frames, _, height, width = lat_ref.shape
    gain = spread(gain_ref[...], width)
    bias, gain_mid = spread(bias_ref[...], width), spread(gain_mid_ref[...], width)
    mid_ref[0] = bias
    mid_ref[1] = gain_mid
    for f in range(frames):
        norm_frame(lat_ref, f, range(height - 2), gain, xs_ref)
    for k in range(4):
        rows = inner_rows(xs_ref, wt_ref, keep_ref, edge_ref, frames - 2 + k, width)
        for h, total in enumerate(rows, -1):
            if h < 1:
                part_ref[k, :, (h + 1) * width : (h + 2) * width] = total
            else:
                if k < 2:
                    total = act_rows(total, h, height, bias, gain_mid)
                early_ref[k, :, (h - 1) * width : h * width] = total.astype(BF16)


def head_kernel(keep_ref, xs_ref, wt_ref, edge_ref, weight_ref, head_ref, w_ref):
    frames, outs, _ = head_ref.shape
    width = edge_ref.shape[2] // 3
    for i in range(3):
        w_ref[i * outs : (i + 1) * outs, :] = fold_taps(weight_ref, i, range(3))
    for out in range(frames):
        rows = inner_rows(xs_ref, wt_ref, keep_ref, edge_ref, out, width)
        for n, total in enumerate(rows):
            head_ref[out, :, n * width : (n + 1) * width] = total


def act_rows(total, h, height, bias, gain):
    hidden = (total + bias).astype(BF16).astype(F32)
    act = silu_norm(hidden, gain)
    if h == -1:
        return jnp.where(lax.axis_index("rows") > 0, act, 0.0)
    if h == height - 1:
        return jnp.where(lax.axis_index("rows") == lax.axis_size("rows") - 1, act, 0.0)
    return act


def late_kernel(part_ref, got_ref, mid_ref, late_ref):
    width = got_ref.shape[2] // 2
    frames = got_ref.shape[0] - 2
    bias, gain = mid_ref[0], mid_ref[1]
    for k in range(4):
        for h in (-1, 0):
            cols = pl.ds((h + 1) * width, width)
            total = part_ref[k, :, cols] + got_ref[frames - 2 + k, :, cols].astype(F32)
            if k < 2:
                total = act_rows(total, h, 0, bias, gain)
            late_ref[k, :, cols] = total.astype(BF16)


def act_taps(mine_ref, before_ref, sums, rows, height, bias, gain, frames, xs_ref):
    outs = mine_ref.shape[1]
    width = mine_ref.shape[2] // len(rows)
    for s in range(-2, frames):
        for n, h in enumerate(rows):
            cols = pl.ds(n * width, width)
            if s < 0:
                act = before_ref[s + 2, :, cols].astype(F32)
            elif s >= frames - 2:
                act = mine_ref[s - frames + 2, :, cols].astype(F32)
            else:
                total = sums(s, h)
                if s < 2:
                    total = total + before_ref[2 + s, :, cols].astype(F32)
                act = act_rows(total, h, height, bias, gain)
            for j, tap in enumerate(column_taps(act)):
                xs_ref[pl.ds(((s + 2) * 3 + j) * outs, outs), cols] = tap


def edge_kernel(keep_ref, head_ref, got_ref, mine_ref, before_ref, mid_ref, w_ref, down_ref, edge_ref, xs_ref):
    width = got_ref.shape[2] // 2
    frames = got_ref.shape[0] - 2
    bias, gain = mid_ref[0], mid_ref[1]

    def sums(s, h):
        cols = pl.ds((h + 1) * width, width)
        return head_ref[s, :, cols] + got_ref[s, :, cols].astype(F32)

    act_taps(mine_ref, before_ref, sums, (-1, 0), 0, bias, gain, frames, xs_ref)
    for out in range(frames):
        y0, y1, y2 = conv_frame(xs_ref, w_ref, keep_ref, out, 2)
        down_ref[out, :, :width] = y2[:, :width].astype(BF16)
        down_ref[out, :, width:] = (y1[:, :width] + y2[:, width:]).astype(BF16)
        edge_ref[out, :, :width] = y0[:, :width] + y1[:, width:]
        edge_ref[out, :, width:] = y0[:, width:]


def body_kernel(keep_ref, head_ref, mine_ref, before_ref, w_ref, edge_ref, mid_ref, lat_ref, skip_ref, bias_mid_ref, skip_bias_ref, total_ref, xs_ref):
    frames, chans, height, width = lat_ref.shape
    bias, gain = mid_ref[0], mid_ref[1]
    shift = spread(bias_mid_ref[...] + skip_bias_ref[...], width)
    sums = lambda s, h: head_ref[s, :, (h + 1) * width : (h + 2) * width]
    act_taps(mine_ref, before_ref, sums, range(1, height), height, bias, gain, frames, xs_ref)
    skip = skip_ref[...]
    for out in range(frames):
        y0, y1, y2 = conv_frame(xs_ref, w_ref, keep_ref, out, 2)
        short = dot(skip, lat_ref[out].reshape(chans, height * width))
        for r in range(height):
            cols = pl.ds(r * width, width)
            total = short[:, r * width : (r + 1) * width] + shift
            for tap, row in ((y0, r - 1), (y1, r), (y2, r + 1)):
                if 1 <= row < height:
                    total = total + tap[:, (row - 1) * width : row * width]
            if r < 2:
                total = total + edge_ref[out, :, cols]
            total_ref[out, :, cols] = total


def last_kernel(total_ref, below_ref, out_ref):
    frames, outs, height, width = out_ref.shape
    for f in range(frames):
        rows = [total_ref[f, :, r * width : (r + 1) * width] for r in range(height)]
        for n in range(2):
            rows[height - 2 + n] = rows[height - 2 + n] + below_ref[f, :, n * width : (n + 1) * width].astype(F32)
        out_ref[f] = jnp.concatenate(rows, axis=1).reshape(outs, height, width).astype(BF16)


def call(kernel, shapes, operands, flops, places=(), scratch=()):
    moved = sum(x.size * x.dtype.itemsize for x in operands) + sum(s.size * s.dtype.itemsize for s in shapes)
    single = len(shapes) == 1
    places = list(places) + [VMEM] * (len(operands) - len(places))
    return pl.pallas_call(
        kernel,
        out_shape=shapes[0] if single else tuple(shapes),
        in_specs=places,
        out_specs=VMEM if single else tuple(VMEM for _ in shapes),
        scratch_shapes=list(scratch),
        cost_estimate=pl.CostEstimate(flops=flops, bytes_accessed=moved, transcendentals=0),
        compiler_params=pltpu.CompilerParams(vmem_limit_bytes=20 << 20),
    )(*operands)


def moved_by(block, axis, distance):
    devices = range(lax.axis_size(axis))
    return lax.ppermute(block, axis, [(i, i + distance) for i in devices if i + distance in devices])


def shards(latent, clip_ids, gain_in, conv_in, bias_in, gain_mid, conv_mid, bias_mid, skip_weight, skip_bias):
    frames, chans, height, width = latent.shape
    outs = conv_in.shape[3]
    shape = jax.ShapeDtypeStruct
    row = lambda v: v.reshape(1, -1)
    deep, deep_mid, tall = 3 * chans, 3 * outs, 3 * outs
    work = 2 * tall * 3 * deep * frames * width
    wt, up, edge, lat, keep = call(
        first_kernel,
        [
            shape((tall, 3 * deep), BF16),
            shape((frames + 2, outs, 2 * width), BF16),
            shape((frames + 2, outs, 3 * width), F32),
            shape(latent.shape, BF16),
            shape((2 * (frames + 2), 16, width), BF16),
        ],
        tuple(pltpu.with_memory_space_constraint(x, pltpu.HBM) for x in (clip_ids, latent, conv_in, row(gain_in))),
        work * 2,
        [HBM] * 4,
        [
            pltpu.VMEM((frames * deep, 2 * width), BF16),
            pltpu.VMEM(conv_in.shape, BF16),
            pltpu.VMEM((1, chans), F32),
            pltpu.SMEM(clip_ids.shape, jnp.int32),
            pltpu.SemaphoreType.DMA((frames + 3,)),
        ],
    )
    got = moved_by(up, "rows", 1)
    part, early, xs, mid = call(
        inner_kernel,
        [
            shape((4, outs, 2 * width), F32),
            shape((4, outs, (height - 1) * width), BF16),
            shape((frames * deep, (height - 2) * width), BF16),
            shape((2, outs, width), F32),
        ],
        (keep, lat, row(gain_in), wt, edge, row(bias_in), row(gain_mid)),
        work * (height - 2),
    )
    before_early = moved_by(early, "tm", 1)
    head, w_mid = call(
        head_kernel,
        [shape((frames - 2, outs, (height + 1) * width), F32), shape((tall, 3 * deep_mid), BF16)],
        (keep, xs, wt, edge, conv_mid),
        work,
    )
    late = call(late_kernel, [shape((4, outs, 2 * width), BF16)], (part, got, mid), 1000)
    before_late = moved_by(late, "tm", 1)
    down, edge_mid = call(
        edge_kernel,
        [shape((frames, outs, 2 * width), BF16), shape((frames, outs, 2 * width), F32)],
        (keep, head, got, late, before_late, mid, w_mid),
        work,
        scratch=[pltpu.VMEM(((frames + 2) * deep_mid, 2 * width), BF16)],
    )
    below = moved_by(down, "rows", -1)
    total = call(
        body_kernel,
        [shape((frames, outs, height * width), F32)],
        (keep, head, early, before_early, w_mid, edge_mid, mid, lat, skip_weight, row(bias_mid), row(skip_bias)),
        work * (height - 1) // 2,
        scratch=[pltpu.VMEM(((frames + 2) * deep_mid, (height - 1) * width), BF16)],
    )
    return call(last_kernel, [shape((frames, outs, height, width), BF16)], (total, below), 1000)


def solution(mesh):
    return jax.shard_map(
        shards,
        mesh=mesh,
        in_specs=(P("tm", None, "rows", None), P(), P(), P(), P(), P(), P(), P(), P(), P()),
        out_specs=P("tm", None, "rows", None),
        check_vma=False,
    )
```

```python
import jax
import jax.numpy as jnp
from jax import lax
from jax.experimental import pallas as pl
from jax.experimental.pallas import tpu as pltpu
from jax.sharding import PartitionSpec as P


F32 = jnp.float32
BF16 = jnp.bfloat16
VMEM = pl.BlockSpec(memory_space=pltpu.VMEM)
HBM = pl.BlockSpec(memory_space=pltpu.HBM)


def silu_norm(values, gain):
    mean_sq = jnp.mean(values * values, axis=0, keepdims=True)
    scaled = values * lax.rsqrt(mean_sq + 1e-06) * gain
    return scaled / (1.0 + jnp.exp(-scaled))


def column_taps(act):
    lane = lax.broadcasted_iota(jnp.int32, act.shape, 1)
    width = act.shape[1]
    left = jnp.where(lane == 0, 0.0, pltpu.roll(act, 1, 1))
    right = jnp.where(lane == width - 1, 0.0, pltpu.roll(act, width - 1, 1))
    return left.astype(BF16), act.astype(BF16), right.astype(BF16)


def spread(vector, width):
    return jnp.broadcast_to(vector, (width, vector.shape[1])).T


def kept(clip_ref, frame, back):
    final = clip_ref.shape[0] - 1
    here = clip_ref[jnp.clip(frame, 0, final)]
    there = clip_ref[jnp.clip(frame - back, 0, final)]
    return (frame - back >= 0) & (here == there)


def fold_taps(weight_ref, row_tap, taps):
    return jnp.concatenate([weight_ref[t, row_tap, j] for t in taps for j in range(3)], axis=1)


def dot(a, b):
    return jnp.dot(a, b, preferred_element_type=F32)


def norm_frame(lat_ref, frame, rows, gain, xs_ref):
    _, chans, height, width = lat_ref.shape
    values = lat_ref[frame].reshape(chans, height * width)
    for n, r in enumerate(rows):
        act = silu_norm(values[:, r * width : (r + 1) * width].astype(F32), gain)
        for j, tap in enumerate(column_taps(act)):
            xs_ref[pl.ds((frame * 3 + j) * chans, chans), n * width : (n + 1) * width] = tap


def conv_frame(xs_ref, wt_ref, keep_ref, out, lag):
    depth = wt_ref.shape[1] // 3
    columns = xs_ref.shape[1]
    taps = [t for t in range(3) if 0 <= out - 2 + t + lag < xs_ref.shape[0] // depth]
    blocks = []
    for t in taps:
        block = xs_ref[pl.ds((out - 2 + t + lag) * depth, depth), :]
        if t < 2:
            keep = keep_ref[2 * out + 1 - t]
            high, width = keep.shape
            keep = jnp.concatenate([keep] * (columns // width), axis=1)
            block = (block.reshape(depth // high, high, columns) * keep[None]).reshape(depth, columns)
        blocks.append(block)
    first = taps[0] * depth
    spare = first % 128
    if spare:
        blocks.insert(0, jnp.zeros((spare, columns), BF16))
    weight = wt_ref[:, first - spare : (taps[-1] + 1) * depth]
    outs = weight.shape[0] // 3
    y = dot(weight, blocks[0] if len(blocks) == 1 else jnp.concatenate(blocks, axis=0))
    return [y[i * outs : (i + 1) * outs] for i in range(3)]


def first_kernel(clip_hbm, lat_hbm, weight_hbm, gain_hbm, wt_ref, up_ref, cross_ref, edge_ref, lat_ref, keep_ref, xs_ref, weight_ref, gain_ref, clip_ref, sems):
    frames, _, height, width = lat_ref.shape
    outs = weight_ref.shape[3]
    start = lax.axis_index("tm") * frames
    pairs = [(gain_hbm, gain_ref)] + [(lat_hbm.at[f], lat_ref.at[f]) for f in range(frames)] + [(clip_hbm, clip_ref)]
    pairs += [(weight_hbm, weight_ref)]
    copies = [pltpu.make_async_copy(a, b, sems.at[n]) for n, (a, b) in enumerate(pairs)]
    for copy in copies:
        copy.start()
    copies[0].wait()
    gain = spread(gain_ref[...], width)
    for f in range(frames):
        copies[1 + f].wait()
        norm_frame(lat_ref, f, (height - 2, height - 1), gain, xs_ref)
    copies[1 + frames].wait()
    for out in range(frames + 2):
        for back in (1, 2):
            flag = jnp.where(kept(clip_ref, start + out, back), 1.0, 0.0)
            keep_ref[2 * out + back - 1] = jnp.full(keep_ref.shape[1:], flag, F32).astype(BF16)

    def message(out):
        y0, y1, y2 = conv_frame(xs_ref, wt_ref, keep_ref, out, 0)
        far = y0[:, :width] + y1[:, width:]
        for ref, place in ((up_ref, out), (cross_ref, out - frames + 2)):
            if 0 <= place < ref.shape[0]:
                ref[place, :, :width] = far.astype(BF16)
                ref[place, :, width:] = y0[:, width:].astype(BF16)
        edge_ref[out, :, :width] = y2[:, :width]
        edge_ref[out, :, width : 2 * width] = y1[:, :width] + y2[:, width:]
        edge_ref[out, :, 2 * width :] = far

    for copy in copies[2 + frames :]:
        copy.wait()
    for i in range(3):
        wt_ref[i * outs : (i + 1) * outs, :] = fold_taps(weight_ref, i, range(3))
    for out in range(frames + 2):
        message(out)


def inner_rows(xs_ref, wt_ref, keep_ref, edge_ref, out, width):
    inner = xs_ref.shape[1] // width
    y0, y1, y2 = conv_frame(xs_ref, wt_ref, keep_ref, out, 0)
    rows = []
    for h in range(-1, inner + 2):
        total = None
        for tap, row in ((y0, h - 1), (y1, h), (y2, h + 1)):
            if 0 <= row < inner:
                term = tap[:, row * width : (row + 1) * width]
                total = term if total is None else total + term
        if h >= inner - 1:
            e = h - inner + 1
            term = edge_ref[out, :, e * width : (e + 1) * width]
            total = term if total is None else total + term
        rows.append(total)
    return rows


def inner_kernel(keep_ref, lat_ref, gain_ref, wt_ref, edge_ref, bias_ref, gain_mid_ref, part_ref, near_ref, early_ref, xs_ref, mid_ref):
    frames, _, height, width = lat_ref.shape
    gain = spread(gain_ref[...], width)
    bias, gain_mid = spread(bias_ref[...], width), spread(gain_mid_ref[...], width)
    mid_ref[0] = bias
    mid_ref[1] = gain_mid
    for f in range(frames):
        norm_frame(lat_ref, f, range(height - 2), gain, xs_ref)
    for k in range(4):
        rows = inner_rows(xs_ref, wt_ref, keep_ref, edge_ref, frames - 2 + k, width)
        for h, total in enumerate(rows, -1):
            if h < 1:
                cols = pl.ds((h + 1) * width, width)
                near_ref[k, :, cols] = total.astype(BF16)
                if k < 2:
                    part_ref[k, :, cols] = total
            else:
                if k < 2:
                    total = act_rows(total, h, height, bias, gain_mid)
                early_ref[k, :, (h - 1) * width : h * width] = total.astype(BF16)


def head_kernel(keep_ref, xs_ref, wt_ref, edge_ref, weight_ref, head_ref, w_ref):
    frames, outs, _ = head_ref.shape
    width = edge_ref.shape[2] // 3
    for i in range(3):
        w_ref[i * outs : (i + 1) * outs, :] = fold_taps(weight_ref, i, range(3))
    for out in range(frames):
        rows = inner_rows(xs_ref, wt_ref, keep_ref, edge_ref, out, width)
        for n, total in enumerate(rows):
            head_ref[out, :, n * width : (n + 1) * width] = total


def act_rows(total, h, height, bias, gain):
    hidden = (total + bias).astype(BF16).astype(F32)
    act = silu_norm(hidden, gain)
    if h == -1:
        return jnp.where(lax.axis_index("rows") > 0, act, 0.0)
    if h == height - 1:
        return jnp.where(lax.axis_index("rows") == lax.axis_size("rows") - 1, act, 0.0)
    return act


def act_taps(act_of, rows, frames, xs_ref, width):
    outs = xs_ref.shape[0] // (3 * (frames + 2))
    for s in range(-2, frames):
        for n, h in enumerate(rows):
            for j, tap in enumerate(column_taps(act_of(s, h))):
                xs_ref[pl.ds(((s + 2) * 3 + j) * outs, outs), n * width : (n + 1) * width] = tap


def edge_kernel(keep_ref, head_ref, part_ref, got_ref, before_ref, cross_ref, mid_ref, w_ref, down_ref, edge_ref, xs_ref):
    width = got_ref.shape[2] // 2
    frames = got_ref.shape[0]
    bias, gain = mid_ref[0], mid_ref[1]

    def act_of(s, h):
        cols = pl.ds((h + 1) * width, width)
        total = None
        if s >= 0:
            own = part_ref[s - frames + 2, :, cols] if s >= frames - 2 else head_ref[s, :, cols]
            total = own + got_ref[s, :, cols].astype(F32)
        if s < 2:
            sent = before_ref[s + 2, :, cols].astype(F32) + cross_ref[s + 2, :, cols].astype(F32)
            total = sent if total is None else total + sent
        return act_rows(total, h, 0, bias, gain)

    act_taps(act_of, (-1, 0), frames, xs_ref, width)
    for out in range(frames):
        y0, y1, y2 = conv_frame(xs_ref, w_ref, keep_ref, out, 2)
        down_ref[out, :, :width] = y2[:, :width].astype(BF16)
        down_ref[out, :, width:] = (y1[:, :width] + y2[:, width:]).astype(BF16)
        edge_ref[out, :, :width] = y0[:, :width] + y1[:, width:]
        edge_ref[out, :, width:] = y0[:, width:]


def body_kernel(keep_ref, head_ref, mine_ref, before_ref, w_ref, edge_ref, mid_ref, lat_ref, skip_ref, bias_mid_ref, skip_bias_ref, total_ref, xs_ref):
    frames, chans, height, width = lat_ref.shape
    bias, gain = mid_ref[0], mid_ref[1]
    shift = spread(bias_mid_ref[...] + skip_bias_ref[...], width)

    def act_of(s, h):
        cols = pl.ds((h - 1) * width, width)
        if s < 0:
            return before_ref[s + 2, :, cols].astype(F32)
        if s >= frames - 2:
            return mine_ref[s - frames + 2, :, cols].astype(F32)
        total = head_ref[s, :, (h + 1) * width : (h + 2) * width]
        if s < 2:
            total = total + before_ref[s + 2, :, cols].astype(F32)
        return act_rows(total, h, height, bias, gain)

    act_taps(act_of, range(1, height), frames, xs_ref, width)
    skip = skip_ref[...]
    for out in range(frames):
        y0, y1, y2 = conv_frame(xs_ref, w_ref, keep_ref, out, 2)
        short = dot(skip, lat_ref[out].reshape(chans, height * width))
        for r in range(height):
            cols = pl.ds(r * width, width)
            total = short[:, r * width : (r + 1) * width] + shift
            for tap, row in ((y0, r - 1), (y1, r), (y2, r + 1)):
                if 1 <= row < height:
                    total = total + tap[:, (row - 1) * width : row * width]
            if r < 2:
                total = total + edge_ref[out, :, cols]
            total_ref[out, :, cols] = total


def last_kernel(total_ref, below_ref, out_ref):
    frames, outs, height, width = out_ref.shape
    for f in range(frames):
        rows = [total_ref[f, :, r * width : (r + 1) * width] for r in range(height)]
        for n in range(2):
            rows[height - 2 + n] = rows[height - 2 + n] + below_ref[f, :, n * width : (n + 1) * width].astype(F32)
        out_ref[f] = jnp.concatenate(rows, axis=1).reshape(outs, height, width).astype(BF16)


def call(kernel, shapes, operands, flops, places=(), scratch=()):
    moved = sum(x.size * x.dtype.itemsize for x in operands) + sum(s.size * s.dtype.itemsize for s in shapes)
    single = len(shapes) == 1
    places = list(places) + [VMEM] * (len(operands) - len(places))
    return pl.pallas_call(
        kernel,
        out_shape=shapes[0] if single else tuple(shapes),
        in_specs=places,
        out_specs=VMEM if single else tuple(VMEM for _ in shapes),
        scratch_shapes=list(scratch),
        cost_estimate=pl.CostEstimate(flops=flops, bytes_accessed=moved, transcendentals=0),
        compiler_params=pltpu.CompilerParams(vmem_limit_bytes=20 << 20),
    )(*operands)


def moved_by(block, axis, distance):
    devices = range(lax.axis_size(axis))
    return lax.ppermute(block, axis, [(i, i + distance) for i in devices if i + distance in devices])


def moved_across(block):
    steps, lines = lax.axis_size("tm"), lax.axis_size("rows")
    route = [(t * lines + i, (t + 1) * lines + i + 1) for t in range(steps - 1) for i in range(lines - 1)]
    return lax.ppermute(block, ("tm", "rows"), route)


def shards(latent, clip_ids, gain_in, conv_in, bias_in, gain_mid, conv_mid, bias_mid, skip_weight, skip_bias):
    frames, chans, height, width = latent.shape
    outs = conv_in.shape[3]
    shape = jax.ShapeDtypeStruct
    row = lambda v: v.reshape(1, -1)
    deep, deep_mid, tall = 3 * chans, 3 * outs, 3 * outs
    work = 2 * tall * 3 * deep * frames * width
    wt, up, cross, edge, lat, keep = call(
        first_kernel,
        [
            shape((tall, 3 * deep), BF16),
            shape((frames, outs, 2 * width), BF16),
            shape((4, outs, 2 * width), BF16),
            shape((frames + 2, outs, 3 * width), F32),
            shape(latent.shape, BF16),
            shape((2 * (frames + 2), 16, width), BF16),
        ],
        tuple(pltpu.with_memory_space_constraint(x, pltpu.HBM) for x in (clip_ids, latent, conv_in, row(gain_in))),
        work * 2,
        [HBM] * 4,
        [
            pltpu.VMEM((frames * deep, 2 * width), BF16),
            pltpu.VMEM(conv_in.shape, BF16),
            pltpu.VMEM((1, chans), F32),
            pltpu.SMEM(clip_ids.shape, jnp.int32),
            pltpu.SemaphoreType.DMA((frames + 3,)),
        ],
    )
    got = moved_by(up, "rows", 1)
    cross_got = moved_across(cross)
    part, near, early, xs, mid = call(
        inner_kernel,
        [
            shape((2, outs, 2 * width), F32),
            shape((4, outs, 2 * width), BF16),
            shape((4, outs, (height - 1) * width), BF16),
            shape((frames * deep, (height - 2) * width), BF16),
            shape((2, outs, width), F32),
        ],
        (keep, lat, row(gain_in), wt, edge, row(bias_in), row(gain_mid)),
        work * (height - 2),
    )
    before_near = moved_by(near, "tm", 1)
    before_early = moved_by(early, "tm", 1)
    head, w_mid = call(
        head_kernel,
        [shape((frames - 2, outs, (height + 1) * width), F32), shape((tall, 3 * deep_mid), BF16)],
        (keep, xs, wt, edge, conv_mid),
        work,
    )
    down, edge_mid = call(
        edge_kernel,
        [shape((frames, outs, 2 * width), BF16), shape((frames, outs, 2 * width), F32)],
        (keep, head, part, got, before_near, cross_got, mid, w_mid),
        work,
        scratch=[pltpu.VMEM(((frames + 2) * deep_mid, 2 * width), BF16)],
    )
    below = moved_by(down, "rows", -1)
    total = call(
        body_kernel,
        [shape((frames, outs, height * width), F32)],
        (keep, head, early, before_early, w_mid, edge_mid, mid, lat, skip_weight, row(bias_mid), row(skip_bias)),
        work * (height - 1) // 2,
        scratch=[pltpu.VMEM(((frames + 2) * deep_mid, (height - 1) * width), BF16)],
    )
    return call(last_kernel, [shape((frames, outs, height, width), BF16)], (total, below), 1000)


def solution(mesh):
    return jax.shard_map(
        shards,
        mesh=mesh,
        in_specs=(P("tm", None, "rows", None), P(), P(), P(), P(), P(), P(), P(), P(), P()),
        out_specs=P("tm", None, "rows", None),
        check_vma=False,
    )
```

```python
import jax
import jax.numpy as jnp
from jax import lax
from jax.experimental import pallas as pl
from jax.experimental.pallas import tpu as pltpu
from jax.sharding import PartitionSpec as P


F32 = jnp.float32
BF16 = jnp.bfloat16
VMEM = pl.BlockSpec(memory_space=pltpu.VMEM)
HBM = pl.BlockSpec(memory_space=pltpu.HBM)


def silu_norm(values, gain):
    mean_sq = jnp.mean(values * values, axis=0, keepdims=True)
    scaled = values * lax.rsqrt(mean_sq + 1e-06) * gain
    return scaled / (1.0 + jnp.exp(-scaled))


def column_taps(act):
    lane = lax.broadcasted_iota(jnp.int32, act.shape, 1)
    width = act.shape[1]
    left = jnp.where(lane == 0, 0.0, pltpu.roll(act, 1, 1))
    right = jnp.where(lane == width - 1, 0.0, pltpu.roll(act, width - 1, 1))
    return left.astype(BF16), act.astype(BF16), right.astype(BF16)


def spread(vector, width):
    return jnp.broadcast_to(vector, (width, vector.shape[1])).T


def kept(clip_ref, frame, back):
    final = clip_ref.shape[0] - 1
    here = clip_ref[jnp.clip(frame, 0, final)]
    there = clip_ref[jnp.clip(frame - back, 0, final)]
    return (frame - back >= 0) & (here == there)


def fold_taps(weight_ref, row_tap, taps):
    return jnp.concatenate([weight_ref[t, row_tap, j] for t in taps for j in range(3)], axis=1)


def dot(a, b):
    return jnp.dot(a, b, preferred_element_type=F32)


def norm_frame(lat_ref, frame, rows, gain, xs_ref):
    _, chans, height, width = lat_ref.shape
    values = lat_ref[frame].reshape(chans, height * width)
    for n, r in enumerate(rows):
        act = silu_norm(values[:, r * width : (r + 1) * width].astype(F32), gain)
        for j, tap in enumerate(column_taps(act)):
            xs_ref[pl.ds((frame * 3 + j) * chans, chans), n * width : (n + 1) * width] = tap


def conv_frame(xs_ref, wt_ref, keep_ref, out, lag):
    depth = wt_ref.shape[1] // 3
    columns = xs_ref.shape[1]
    taps = [t for t in range(3) if 0 <= out - 2 + t + lag < xs_ref.shape[0] // depth]
    blocks = []
    for t in taps:
        block = xs_ref[pl.ds((out - 2 + t + lag) * depth, depth), :]
        if t < 2:
            keep = keep_ref[2 * out + 1 - t]
            high, width = keep.shape
            keep = jnp.concatenate([keep] * (columns // width), axis=1)
            block = (block.reshape(depth // high, high, columns) * keep[None]).reshape(depth, columns)
        blocks.append(block)
    first = taps[0] * depth
    spare = first % 128
    if spare:
        blocks.insert(0, jnp.zeros((spare, columns), BF16))
    weight = wt_ref[:, first - spare : (taps[-1] + 1) * depth]
    outs = weight.shape[0] // 3
    y = dot(weight, blocks[0] if len(blocks) == 1 else jnp.concatenate(blocks, axis=0))
    return [y[i * outs : (i + 1) * outs] for i in range(3)]


def first_kernel(clip_hbm, lat_hbm, weight_hbm, gain_hbm, wt_ref, up_ref, cross_ref, edge_ref, lat_ref, keep_ref, xs_ref, weight_ref, gain_ref, clip_ref, sems):
    frames, _, height, width = lat_ref.shape
    outs = weight_ref.shape[3]
    start = lax.axis_index("tm") * frames
    pairs = [(gain_hbm, gain_ref)] + [(lat_hbm.at[f], lat_ref.at[f]) for f in range(frames)] + [(clip_hbm, clip_ref)]
    pairs += [(weight_hbm, weight_ref)]
    copies = [pltpu.make_async_copy(a, b, sems.at[n]) for n, (a, b) in enumerate(pairs)]
    for copy in copies:
        copy.start()
    copies[0].wait()
    gain = spread(gain_ref[...], width)
    for f in range(frames):
        copies[1 + f].wait()
        norm_frame(lat_ref, f, (height - 2, height - 1), gain, xs_ref)
    copies[1 + frames].wait()
    for out in range(frames + 2):
        for back in (1, 2):
            flag = jnp.where(kept(clip_ref, start + out, back), 1.0, 0.0)
            keep_ref[2 * out + back - 1] = jnp.full(keep_ref.shape[1:], flag, F32).astype(BF16)

    def message(out):
        y0, y1, y2 = conv_frame(xs_ref, wt_ref, keep_ref, out, 0)
        far = y0[:, :width] + y1[:, width:]
        for ref, place in ((up_ref, out), (cross_ref, out - frames + 2)):
            if 0 <= place < ref.shape[0]:
                ref[place, :, :width] = far.astype(BF16)
                ref[place, :, width:] = y0[:, width:].astype(BF16)
        edge_ref[out, :, :width] = y2[:, :width]
        edge_ref[out, :, width : 2 * width] = y1[:, :width] + y2[:, width:]
        edge_ref[out, :, 2 * width :] = far

    for copy in copies[2 + frames :]:
        copy.wait()
    for i in range(3):
        wt_ref[i * outs : (i + 1) * outs, :] = fold_taps(weight_ref, i, range(3))
    for out in range(frames + 2):
        message(out)


def inner_rows(xs_ref, wt_ref, keep_ref, edge_ref, out, width):
    inner = xs_ref.shape[1] // width
    y0, y1, y2 = conv_frame(xs_ref, wt_ref, keep_ref, out, 0)
    rows = []
    for h in range(-1, inner + 2):
        total = None
        for tap, row in ((y0, h - 1), (y1, h), (y2, h + 1)):
            if 0 <= row < inner:
                term = tap[:, row * width : (row + 1) * width]
                total = term if total is None else total + term
        if h >= inner - 1:
            e = h - inner + 1
            term = edge_ref[out, :, e * width : (e + 1) * width]
            total = term if total is None else total + term
        rows.append(total)
    return rows


def inner_kernel(keep_ref, lat_ref, gain_ref, wt_ref, edge_ref, bias_ref, gain_mid_ref, part_ref, near_ref, early_ref, xs_ref, mid_ref):
    frames, _, height, width = lat_ref.shape
    gain = spread(gain_ref[...], width)
    bias, gain_mid = spread(bias_ref[...], width), spread(gain_mid_ref[...], width)
    mid_ref[0] = bias
    mid_ref[1] = gain_mid
    for f in range(frames):
        norm_frame(lat_ref, f, range(height - 2), gain, xs_ref)
    for k in range(4):
        rows = inner_rows(xs_ref, wt_ref, keep_ref, edge_ref, frames - 2 + k, width)
        for h, total in enumerate(rows, -1):
            if h < 1:
                cols = pl.ds((h + 1) * width, width)
                near_ref[k, :, cols] = total.astype(BF16)
                if k < 2:
                    part_ref[k, :, cols] = total
            else:
                if k < 2:
                    total = act_rows(total, h, height, bias, gain_mid)
                early_ref[k, :, (h - 1) * width : h * width] = total.astype(BF16)


def head_kernel(keep_ref, xs_ref, wt_ref, edge_ref, weight_ref, head_ref, w_ref):
    frames, outs, _ = head_ref.shape
    width = edge_ref.shape[2] // 3
    for i in range(3):
        w_ref[i * outs : (i + 1) * outs, :] = fold_taps(weight_ref, i, range(3))
    for out in range(frames):
        rows = inner_rows(xs_ref, wt_ref, keep_ref, edge_ref, out, width)
        for n, total in enumerate(rows):
            head_ref[out, :, n * width : (n + 1) * width] = total


def act_rows(total, h, height, bias, gain):
    hidden = (total + bias).astype(BF16).astype(F32)
    act = silu_norm(hidden, gain)
    if h == -1:
        return jnp.where(lax.axis_index("rows") > 0, act, 0.0)
    if h == height - 1:
        return jnp.where(lax.axis_index("rows") == lax.axis_size("rows") - 1, act, 0.0)
    return act


def act_taps(act_of, rows, frames, xs_ref, width):
    outs = xs_ref.shape[0] // (3 * (frames + 2))
    for s in range(-2, frames):
        for n, h in enumerate(rows):
            for j, tap in enumerate(column_taps(act_of(s, h))):
                xs_ref[pl.ds(((s + 2) * 3 + j) * outs, outs), n * width : (n + 1) * width] = tap


def edge_kernel(keep_ref, head_ref, part_ref, got_ref, before_ref, cross_ref, mid_ref, w_ref, down_ref, edge_ref, xs_ref):
    width = got_ref.shape[2] // 2
    frames = got_ref.shape[0]
    bias, gain = mid_ref[0], mid_ref[1]

    def act_of(s, h):
        cols = pl.ds((h + 1) * width, width)
        total = None
        if s >= 0:
            own = part_ref[s - frames + 2, :, cols] if s >= frames - 2 else head_ref[s, :, cols]
            total = own + got_ref[s, :, cols].astype(F32)
        if s < 2:
            sent = before_ref[s + 2, :, cols].astype(F32) + cross_ref[s + 2, :, cols].astype(F32)
            total = sent if total is None else total + sent
        return act_rows(total, h, 0, bias, gain)

    act_taps(act_of, (-1, 0), frames, xs_ref, width)
    for out in range(frames):
        y0, y1, y2 = conv_frame(xs_ref, w_ref, keep_ref, out, 2)
        down_ref[out, :, :width] = y2[:, :width].astype(BF16)
        down_ref[out, :, width:] = (y1[:, :width] + y2[:, width:]).astype(BF16)
        edge_ref[out, :, :width] = y0[:, :width] + y1[:, width:]
        edge_ref[out, :, width:] = y0[:, width:]


def body_kernel(keep_ref, head_ref, mine_ref, before_ref, w_ref, edge_ref, mid_ref, lat_ref, skip_ref, bias_mid_ref, skip_bias_ref, total_ref, xs_ref):
    frames, chans, height, width = lat_ref.shape
    bias, gain = mid_ref[0], mid_ref[1]
    shift = spread(bias_mid_ref[...] + skip_bias_ref[...], width)

    def act_of(s, h):
        cols = pl.ds((h - 1) * width, width)
        if s < 0:
            return before_ref[s + 2, :, cols].astype(F32)
        if s >= frames - 2:
            return mine_ref[s - frames + 2, :, cols].astype(F32)
        total = head_ref[s, :, (h + 1) * width : (h + 2) * width]
        if s < 2:
            total = total + before_ref[s + 2, :, cols].astype(F32)
        return act_rows(total, h, height, bias, gain)

    act_taps(act_of, range(1, height), frames, xs_ref, width)
    skip = skip_ref[...]
    for out in range(frames):
        y0, y1, y2 = conv_frame(xs_ref, w_ref, keep_ref, out, 2)
        short = dot(skip, lat_ref[out].reshape(chans, height * width))
        for r in range(height):
            cols = pl.ds(r * width, width)
            total = short[:, r * width : (r + 1) * width] + shift
            for tap, row in ((y0, r - 1), (y1, r), (y2, r + 1)):
                if 1 <= row < height:
                    total = total + tap[:, (row - 1) * width : row * width]
            if r < 2:
                total = total + edge_ref[out, :, cols]
            total_ref[out, :, cols] = total


def last_kernel(total_ref, below_ref, out_hbm, out_ref, sems):
    frames, outs, height, width = out_ref.shape
    copies = []
    for f in range(frames):
        rows = [total_ref[f, :, r * width : (r + 1) * width] for r in range(height)]
        for n in range(2):
            rows[height - 2 + n] = rows[height - 2 + n] + below_ref[f, :, n * width : (n + 1) * width].astype(F32)
        out_ref[f] = jnp.concatenate(rows, axis=1).reshape(outs, height, width).astype(BF16)
        copies.append(pltpu.make_async_copy(out_ref.at[f], out_hbm.at[f], sems.at[f]))
        copies[f].start()
    for copy in copies:
        copy.wait()


def call(kernel, shapes, operands, flops, places=(), scratch=(), result=VMEM):
    moved = sum(x.size * x.dtype.itemsize for x in operands) + sum(s.size * s.dtype.itemsize for s in shapes)
    single = len(shapes) == 1
    places = list(places) + [VMEM] * (len(operands) - len(places))
    return pl.pallas_call(
        kernel,
        out_shape=shapes[0] if single else tuple(shapes),
        in_specs=places,
        out_specs=result if single else tuple(VMEM for _ in shapes),
        scratch_shapes=list(scratch),
        cost_estimate=pl.CostEstimate(flops=flops, bytes_accessed=moved, transcendentals=0),
        compiler_params=pltpu.CompilerParams(vmem_limit_bytes=20 << 20),
    )(*operands)


def moved_by(block, axis, distance):
    devices = range(lax.axis_size(axis))
    return lax.ppermute(block, axis, [(i, i + distance) for i in devices if i + distance in devices])


def moved_across(block):
    steps, lines = lax.axis_size("tm"), lax.axis_size("rows")
    route = [(t * lines + i, (t + 1) * lines + i + 1) for t in range(steps - 1) for i in range(lines - 1)]
    return lax.ppermute(block, ("tm", "rows"), route)


def shards(latent, clip_ids, gain_in, conv_in, bias_in, gain_mid, conv_mid, bias_mid, skip_weight, skip_bias):
    frames, chans, height, width = latent.shape
    outs = conv_in.shape[3]
    shape = jax.ShapeDtypeStruct
    row = lambda v: v.reshape(1, -1)
    deep, deep_mid, tall = 3 * chans, 3 * outs, 3 * outs
    work = 2 * tall * 3 * deep * frames * width
    wt, up, cross, edge, lat, keep = call(
        first_kernel,
        [
            shape((tall, 3 * deep), BF16),
            shape((frames, outs, 2 * width), BF16),
            shape((4, outs, 2 * width), BF16),
            shape((frames + 2, outs, 3 * width), F32),
            shape(latent.shape, BF16),
            shape((2 * (frames + 2), 16, width), BF16),
        ],
        tuple(pltpu.with_memory_space_constraint(x, pltpu.HBM) for x in (clip_ids, latent, conv_in, row(gain_in))),
        work * 2,
        [HBM] * 4,
        [
            pltpu.VMEM((frames * deep, 2 * width), BF16),
            pltpu.VMEM(conv_in.shape, BF16),
            pltpu.VMEM((1, chans), F32),
            pltpu.SMEM(clip_ids.shape, jnp.int32),
            pltpu.SemaphoreType.DMA((frames + 3,)),
        ],
    )
    got = moved_by(up, "rows", 1)
    cross_got = moved_across(cross)
    part, near, early, xs, mid = call(
        inner_kernel,
        [
            shape((2, outs, 2 * width), F32),
            shape((4, outs, 2 * width), BF16),
            shape((4, outs, (height - 1) * width), BF16),
            shape((frames * deep, (height - 2) * width), BF16),
            shape((2, outs, width), F32),
        ],
        (keep, lat, row(gain_in), wt, edge, row(bias_in), row(gain_mid)),
        work * (height - 2),
    )
    before_near = moved_by(near, "tm", 1)
    before_early = moved_by(early, "tm", 1)
    head, w_mid = call(
        head_kernel,
        [shape((frames - 2, outs, (height + 1) * width), F32), shape((tall, 3 * deep_mid), BF16)],
        (keep, xs, wt, edge, conv_mid),
        work,
    )
    down, edge_mid = call(
        edge_kernel,
        [shape((frames, outs, 2 * width), BF16), shape((frames, outs, 2 * width), F32)],
        (keep, head, part, got, before_near, cross_got, mid, w_mid),
        work,
        scratch=[pltpu.VMEM(((frames + 2) * deep_mid, 2 * width), BF16)],
    )
    below = moved_by(down, "rows", -1)
    total = call(
        body_kernel,
        [shape((frames, outs, height * width), F32)],
        (keep, head, early, before_early, w_mid, edge_mid, mid, lat, skip_weight, row(bias_mid), row(skip_bias)),
        work * (height - 1) // 2,
        scratch=[pltpu.VMEM(((frames + 2) * deep_mid, (height - 1) * width), BF16)],
    )
    return call(
        last_kernel,
        [shape((frames, outs, height, width), BF16)],
        (total, below),
        1000,
        scratch=[pltpu.VMEM((frames, outs, height, width), BF16), pltpu.SemaphoreType.DMA((frames,))],
        result=HBM,
    )


def solution(mesh):
    return jax.shard_map(
        shards,
        mesh=mesh,
        in_specs=(P("tm", None, "rows", None), P(), P(), P(), P(), P(), P(), P(), P(), P()),
        out_specs=P("tm", None, "rows", None),
        check_vma=False,
    )
```
